128 devices in a mesh: req: 8 (over x_lo, y), grp: 16 (over z, x_hi, core).
Axes of the slice: x: 4 (x_hi: 2, x_lo: 2; x = x_hi * 2 + x_lo), y: 4, z: 4, core: 2. Of those that a mesh axis runs over, the one named last changes fastest.
Arguments:
- residual: bfloat16 [8, 16, 128, 4096], P('req', 'grp'), may hold values from -64 to 64
- suffix_proj: bfloat16 [8, 16, 3, 128, 4096], P('req', 'grp'), may hold values from -256 to 256
- prefix_cache: bfloat16 [8, 16, 2, 128, 4096], P('req', 'grp'), may hold values from -8 to 8
- owner_req: int32 [16], replicated, may hold values from 0 to 7, as said below
- lengths: int32 [8, 16], P('req', 'grp'), may hold values from 8 to 128, as said below
- norm_gain: float32 [4096], replicated, may hold values from 0.1 to 1.9
- up_weight: bfloat16 [12288, 4096], P('grp'), may hold values from -0.09375 to 0.09375
- down_weight: bfloat16 [12288, 4096], P('grp'), may hold values from -0.0546875 to 0.0546875
Outputs:
- output: bfloat16 [8, 16, 128, 4096], P('req', 'grp')
The draws below stay inside these ranges and needn't reach their ends.
Inputs may be any that keep to these rules, and one draw needn't show every extreme that they name: owner_req[g] is the req index whose cache block holds group g's prefix. The first lengths[r, g] of the 128 slots of a request are live; in every req index one request fills all 128 slots.
All inputs are finite; a program needn't handle non-finite values.
Results may differ from the reference program's by a relative error of at most 0.014.
Values may be sent and summed in bfloat16 or wider, within the bound.
No kernel may reach another device: no remote copies, remote signals or barrier semaphores. Data moves between devices by JAX's collectives and lax.ppermute only.
A program may use at most 128 MiB of HBM per device.

```python
import math
import jax
import jax.numpy as jnp
from jax import lax

D = 4096
HEADS = 32
HEAD_DIM = 128
UNITS = 12288
SLOTS = 128
PREFIX = 128
N_REQ = 8
N_GRP = 16


def owner_table(key):
    return jax.random.randint(jax.random.fold_in(key, 101), (N_GRP,), 0, N_REQ).astype(jnp.int32)


def prefix_table(key):
    sampled = jnp.clip(jax.random.normal(jax.random.fold_in(key, 202), (N_REQ, N_GRP, 2, PREFIX, D), jnp.float32), -6.0, 6.0)
    return sampled


def suffix_table(key):
    sampled = jnp.clip(jax.random.normal(jax.random.fold_in(key, 303), (N_REQ, N_GRP, 3, SLOTS, D), jnp.float32), -6.0, 6.0)
    return sampled


def draw_owner_req(key, part):
    return owner_table(key)


def draw_prefix_cache(key, part):
    return prefix_table(key).astype(jnp.bfloat16)


def draw_suffix_proj(key, part):
    return suffix_table(key).astype(jnp.bfloat16)


def draw_lengths(key, part):
    sampled = jax.random.randint(jax.random.fold_in(key, 404), (N_REQ, N_GRP), 8, SLOTS + 1)
    full_column = jax.random.randint(jax.random.fold_in(key, 405), (N_REQ,), 0, N_GRP)
    columns = jnp.arange(N_GRP, dtype=jnp.int32)[None, :]
    return jnp.where(columns == full_column[:, None], SLOTS, sampled).astype(jnp.int32)


def draw_residual(key, part):
    sampled = jnp.clip(jax.random.normal(jax.random.fold_in(key, 505), (N_REQ, N_GRP, SLOTS, D), jnp.float32), -6.0, 6.0)
    return sampled.astype(jnp.bfloat16)


def levels(key, dims, split, smallest, high):
    gain, own = 1.0, jax.random.fold_in(key, 6)
    for axis_at, parts in split:
        draws = jnp.exp(jax.random.uniform(jax.random.fold_in(own, axis_at), (parts,), jnp.float32, smallest / len(split), high / len(split)))
        gain = gain * jnp.repeat(draws, dims[axis_at] // parts).reshape([-1 if axis == axis_at else 1 for axis in range(len(dims))])
    return gain


def noise(own_key, dims, scale, reach, pieces=(), kind=jnp.bfloat16):
    values = scale * jax.random.normal(own_key, dims, jnp.float32)
    if pieces:
        values = values * levels(own_key, dims, pieces, -0.22, 0.18)
    return jnp.clip(values, -reach, reach).astype(kind)


def setup_inputs(seed: int = 0) -> dict:
    keys = jax.random.split(jax.random.key(seed), 9)
    residual = draw_residual(jax.random.fold_in(keys[8], 71), 0)
    suffix_proj = draw_suffix_proj(jax.random.fold_in(keys[8], 71), 0)
    prefix_cache = draw_prefix_cache(jax.random.fold_in(keys[8], 71), 0)
    owner_req = draw_owner_req(jax.random.fold_in(keys[8], 71), 0)
    lengths = draw_lengths(jax.random.fold_in(keys[8], 71), 0)
    norm_gain = jnp.clip(1.0 + 0.18 * jax.random.normal(keys[5], (D,), jnp.float32), 0.1, 1.9)
    up_weight = noise(keys[6], (UNITS, D), D ** -0.5, 0.09375, ((0, 16),))
    down_weight = noise(keys[7], (UNITS, D), UNITS ** -0.5, 0.0546875, ((0, 16),))
    return {"residual": residual, "suffix_proj": suffix_proj, "prefix_cache": prefix_cache, "owner_req": owner_req, "lengths": lengths, "norm_gain": norm_gain, "up_weight": up_weight, "down_weight": down_weight}


NORM_EPS = 1e-05

def head_slopes():
    return jnp.exp2(-8.0 * jnp.arange(1, HEADS + 1, dtype=jnp.float32) / HEADS)

def attend(queries, key_rows, value_rows, key_pos, query_pos, causal):
    scores = jnp.einsum('qhe,khe->hqk', queries.astype(jnp.float32), key_rows.astype(jnp.float32))
    scores = scores * (1.0 / math.sqrt(HEAD_DIM))
    offsets = (key_pos[None, :] - query_pos[:, None]).astype(jnp.float32)
    scores = scores + head_slopes()[:, None, None] * offsets[None, :, :]
    if causal:
        scores = jnp.where((key_pos[None, :] <= query_pos[:, None])[None], scores, -jnp.inf)
    row_max = lax.optimization_barrier(jnp.max(scores, axis=2))
    weights = jnp.exp(scores - row_max[:, :, None])
    row_total = lax.optimization_barrier(jnp.sum(weights, axis=2))
    rounded = lax.optimization_barrier(weights.astype(jnp.bfloat16)).astype(jnp.float32)
    context = jnp.einsum('hqk,khe->qhe', rounded, value_rows.astype(jnp.float32))
    return (row_max, row_total, context)

def merge_parts(first, second):
    joint_max = jnp.maximum(first[0], second[0])
    first_scale = jnp.exp(first[0] - joint_max)
    second_scale = jnp.exp(second[0] - joint_max)
    numer = first[2] * first_scale.T[:, :, None] + second[2] * second_scale.T[:, :, None]
    denom = first[1] * first_scale + second[1] * second_scale
    merged = numer / denom.T[:, :, None]
    return merged.reshape(merged.shape[0], merged.shape[1] * merged.shape[2])

def layer_norm(state, norm_gain):
    values = state.astype(jnp.float32)
    center = values - lax.optimization_barrier(jnp.mean(values, axis=-1, keepdims=True))
    spread = lax.optimization_barrier(jnp.mean(center * center, axis=-1, keepdims=True))
    return (center * lax.rsqrt(spread + NORM_EPS) * norm_gain).astype(jnp.bfloat16)

def reference(residual, suffix_proj, prefix_cache, owner_req, lengths, norm_gain, up_weight, down_weight):
    query_pos = PREFIX + jnp.arange(SLOTS, dtype=jnp.int32)
    prefix_pos = jnp.arange(PREFIX, dtype=jnp.int32)

    def one_device(device_index):
        req_index = device_index // N_GRP
        group_index = device_index % N_GRP
        block = suffix_proj[req_index, group_index].reshape(3, SLOTS, HEADS, HEAD_DIM)
        cached = prefix_cache[owner_req[group_index], group_index].reshape(2, PREFIX, HEADS, HEAD_DIM)
        first = attend(block[0], cached[0], cached[1], prefix_pos, query_pos, False)
        second = attend(block[0], block[1], block[2], query_pos, query_pos, True)
        context = merge_parts(first, second)
        return (residual[req_index, group_index].astype(jnp.float32) + context).astype(jnp.bfloat16)
    states = lax.map(one_device, jnp.arange(N_REQ * N_GRP, dtype=jnp.int32))
    token_states = states.reshape(N_REQ * N_GRP * SLOTS, D)
    normed = layer_norm(token_states, norm_gain)
    share = UNITS // N_GRP

    def add_class(class_index, running):
        offset = (class_index * share).astype(jnp.int32)
        up_rows = lax.dynamic_slice_in_dim(up_weight, offset, share, 0)
        down_rows = lax.dynamic_slice_in_dim(down_weight, offset, share, 0)
        preactivation = lax.dot_general(normed, up_rows, (((1,), (1,)), ((), ())), preferred_element_type=jnp.float32)
        hidden = jax.nn.gelu(preactivation, approximate=False).astype(jnp.bfloat16)
        partial_term = jnp.dot(hidden, down_rows, preferred_element_type=jnp.float32).astype(jnp.bfloat16)
        return running + partial_term.astype(jnp.float32)
    mlp_sum = lax.fori_loop(0, N_GRP, add_class, jnp.zeros((N_REQ * N_GRP * SLOTS, D), jnp.float32))
    live = jnp.arange(SLOTS, dtype=jnp.int32)[None, None, :] < lengths[:, :, None]
    combined = states.reshape(N_REQ, N_GRP, SLOTS, D).astype(jnp.float32) + mlp_sum.reshape(N_REQ, N_GRP, SLOTS, D)
    return jnp.where(live[..., None], combined, 0.0).astype(jnp.bfloat16)
```

```python
import functools
import math

import jax
import jax.numpy as jnp
from jax import lax
from jax.experimental import pallas as pl
from jax.experimental.pallas import tpu as pltpu
from jax.sharding import PartitionSpec as P

HEADS = 32
NORM_EPS = 1e-05
AXES = ("req", "grp")
F32, BF16 = jnp.float32, jnp.bfloat16
VMEM_LIMIT = 60 * 1024 * 1024


def pairs(move):
    table = []
    for r in range(8):
        for g in range(16):
            xl, y, z, xh, c = r // 4, r % 4, g // 4, (g // 2) % 2, g % 2
            a, b, d, e, f = move(xl, y, z, xh, c)
            table.append((r * 16 + g, (a * 4 + b % 4) * 16 + (d % 4) * 4 + e * 2 + f))
    return tuple(table)


Z_UP = pairs(lambda xl, y, z, xh, c: (xl, y, z + 1, xh, c))
Z_DOWN = pairs(lambda xl, y, z, xh, c: (xl, y, z - 1, xh, c))
Y_UP = pairs(lambda xl, y, z, xh, c: (xl, y + 1, z, xh, c))
Y_DOWN = pairs(lambda xl, y, z, xh, c: (xl, y - 1, z, xh, c))
X_LOW = pairs(lambda xl, y, z, xh, c: (1 - xl, y, z, xh, c))
X_CUT = pairs(lambda xl, y, z, xh, c: (1 - xl, y, z, 1 - xh, c))
CORE = pairs(lambda xl, y, z, xh, c: (xl, y, z, xh, 1 - c))


def req_offset(dx, dy):
    return pairs(lambda xl, y, z, xh, c: ((xl + dx) % 2, y + dy, z, xh, c))


OFFSETS = tuple((dx, dy) for dx in range(2) for dy in (0, 1, 3, 2))


def send(value, table):
    return lax.ppermute(value, AXES, table)


def vmem():
    return pl.BlockSpec(memory_space=pltpu.VMEM)


def smem():
    return pl.BlockSpec(memory_space=pltpu.SMEM)


def hbm():
    return pl.BlockSpec(memory_space=pl.ANY)


def params():
    return pltpu.CompilerParams(vmem_limit_bytes=VMEM_LIMIT)


def cost(flops, nbytes):
    return pl.CostEstimate(flops=int(flops), bytes_accessed=int(nbytes), transcendentals=0)


def cut_kernel(index_ref, cache_ref, *outs):
    for place, out in enumerate(outs):
        row = pl.multiple_of(index_ref[place] * 32, 32)
        out[...] = cache_ref[pl.ds(row, 32), :]


def cut_slices(index, cache):
    width = cache.shape[1]
    return pl.pallas_call(
        cut_kernel,
        out_shape=[jax.ShapeDtypeStruct((32, width), BF16)] * 8,
        in_specs=[smem(), vmem()],
        out_specs=[vmem()] * 8,
        compiler_params=params(),
        cost_estimate=cost(0, 4 * cache.size),
        name="cut_slices",
    )(index, cache)


def suffix_kernel(slope_ref, proj_ref, context_ref, max_ref, total_ref):
    step = pl.program_id(0)
    row = lax.broadcasted_iota(jnp.int32, (128, 128), 0)
    col = lax.broadcasted_iota(jnp.int32, (128, 128), 1)
    offset = (col - row).astype(F32)
    seen = col <= row
    for j in range(4):
        part = slice(j * 128, (j + 1) * 128)
        scores = lax.dot_general(
            proj_ref[0, :, part], proj_ref[1, :, part], (((1,), (1,)), ((), ())), preferred_element_type=F32
        )
        scores = scores * (1.0 / math.sqrt(128)) + slope_ref[step * 4 + j] * offset
        scores = jnp.where(seen, scores, -jnp.inf)
        top = jnp.max(scores, axis=1, keepdims=True)
        weights = jnp.exp(scores - top)
        total = jnp.sum(weights, axis=1, keepdims=True)
        context_ref[:, part] = jnp.dot(weights.astype(BF16), proj_ref[2, :, part], preferred_element_type=F32)
        max_ref[:, part] = jnp.broadcast_to(top, (128, 128))
        total_ref[:, part] = jnp.broadcast_to(total, (128, 128))


def suffix_part(slopes, proj):
    width = proj.shape[2]
    block = pl.BlockSpec((128, 512), lambda i: (0, i))
    return pl.pallas_call(
        suffix_kernel,
        grid=(width // 512,),
        out_shape=[jax.ShapeDtypeStruct((128, width), F32)] * 3,
        in_specs=[smem(), pl.BlockSpec((3, 128, 512), lambda i: (0, 0, i))],
        out_specs=[block] * 3,
        compiler_params=params(),
        cost_estimate=cost(4 * 128 * 128 * width, 9 * 128 * width * 2),
        name="suffix_part",
    )(slopes, proj)


def prefix_kernel(
    slope_ref, place_ref, query_ref, context_ref, max_ref, total_ref, residual_ref, gain_ref,
    s0, s1, s2, s3, s4, s5, s6, s7, state_ref, normed_ref, cached,
):
    for place, piece in enumerate((s0, s1, s2, s3, s4, s5, s6, s7)):
        start = pl.multiple_of(place_ref[place] * 32, 32)
        cached[pl.ds(start, 32), :] = piece[...]
    row = lax.broadcasted_iota(jnp.int32, (128, 128), 0)
    col = lax.broadcasted_iota(jnp.int32, (128, 128), 1)
    offset = (col - row - 128).astype(F32)

    def head(h, running):
        part = pl.ds(pl.multiple_of(h * 128, 128), 128)
        scores = lax.dot_general(
            query_ref[:, part], cached[0:128, part], (((1,), (1,)), ((), ())), preferred_element_type=F32
        )
        scores = scores * (1.0 / math.sqrt(128)) + slope_ref[h] * offset
        top = jnp.max(scores, axis=1, keepdims=True)
        weights = jnp.exp(scores - top)
        total = jnp.sum(weights, axis=1, keepdims=True)
        context = jnp.dot(weights.astype(BF16), cached[128:256, part], preferred_element_type=F32)
        other = max_ref[:, part]
        joint = jnp.maximum(top, other)
        first, second = jnp.exp(top - joint), jnp.exp(other - joint)
        merged = (first * context + second * context_ref[:, part]) / (
            first * total + second * total_ref[:, part]
        )
        state = (residual_ref[:, part].astype(F32) + merged).astype(BF16)
        state_ref[:, part] = state
        return running + state.astype(F32)

    def heads(i, running):
        for j in range(4):
            running = head(i * 4 + j, running)
        return running

    sums = lax.fori_loop(0, HEADS // 4, heads, jnp.zeros((128, 128), F32))
    width = state_ref.shape[1]
    mean = jnp.sum(sums, axis=1, keepdims=True) * (1.0 / width)
    squares = jnp.zeros((128, 128), F32)
    for h in range(HEADS):
        part = slice(h * 128, (h + 1) * 128)
        center = state_ref[:, part].astype(F32) - mean
        squares = squares + center * center
    spread = lax.rsqrt(jnp.sum(squares, axis=1, keepdims=True) * (1.0 / width) + NORM_EPS)
    for h in range(HEADS):
        part = slice(h * 128, (h + 1) * 128)
        center = state_ref[:, part].astype(F32) - mean
        normed_ref[:, part] = (center * spread * gain_ref[:, part]).astype(BF16)


def prefix_part(slopes, places, query, suffix, residual, gain, pieces):
    width = query.shape[1]
    return pl.pallas_call(
        prefix_kernel,
        out_shape=[jax.ShapeDtypeStruct((128, width), BF16)] * 2,
        in_specs=[smem(), smem()] + [vmem()] * 14,
        out_specs=[vmem()] * 2,
        scratch_shapes=[pltpu.VMEM((256, width), BF16)],
        compiler_params=params(),
        cost_estimate=cost(4 * 128 * 128 * width, 12 * 128 * width * 2),
        name="prefix_part",
    )(slopes, places, query, *suffix, residual, gain.reshape(1, width), *pieces)


UNIT_TILE = 256


def unit_copies(units):
    copies, filled = [], 0
    for up_at, up_row, down_at, down_row, count in units:
        done = 0
        while done < count:
            tile, inside = divmod(filled, UNIT_TILE)
            take = min(count - done, UNIT_TILE - inside)
            copies.append((up_at, up_row + done, take, tile, inside))
            copies.append((down_at, down_row + done, take, tile, UNIT_TILE + inside))
            done += take
            filled += take
    return copies, filled


def ffn_kernel(token_rows, source_count, copies, with_acc, split, *refs):
    tokens = refs[: len(token_rows)]
    sources = refs[len(token_rows) : len(token_rows) + source_count]
    rest = refs[len(token_rows) + source_count :]
    start_ref = rest[0] if with_acc else None
    rest = rest[1:] if with_acc else rest
    out_count = len(split) if split else 1
    outs, (rows_buf, weights, hidden, acc, token_sem, tile_sem, acc_sem) = rest[:out_count], rest[out_count:]
    if not split:
        acc = outs[0]
    total = sum(token_rows)
    width = rows_buf.shape[1]
    moves, at = [], 0
    for i, count in enumerate(token_rows):
        move = pltpu.make_async_copy(tokens[i], rows_buf.at[pl.ds(at, count), :], token_sem.at[i])
        move.start()
        moves.append(move)
        at += count
    for index, row, count, tile, inside in copies:
        pltpu.make_async_copy(
            sources[index].at[pl.ds(row, count), :], weights.at[tile, pl.ds(inside, count), :], tile_sem.at[tile]
        ).start()
    if with_acc:
        begin = pltpu.make_async_copy(start_ref, acc, acc_sem)
        begin.start()
    for move in moves:
        move.wait()
    if with_acc:
        begin.wait()
    else:
        acc[...] = jnp.zeros_like(acc)

    @pl.loop(0, weights.shape[0])
    def _(tile):
        pltpu.make_async_copy(weights.at[tile], weights.at[tile], tile_sem.at[tile]).wait()

        @pl.loop(0, total // 128)
        def _(m):
            rows = pl.ds(pl.multiple_of(m * 128, 128), 128)
            pre = lax.dot_general(
                rows_buf[rows, :], weights[tile, 0:UNIT_TILE, :], (((1,), (1,)), ((), ())),
                preferred_element_type=F32,
            )
            hidden[rows, :] = (0.5 * pre * (1.0 + lax.erf(pre * math.sqrt(0.5)))).astype(BF16)

        @pl.loop(0, width // 512)
        def _(n):
            cols = pl.ds(pl.multiple_of(n * 512, 512), 512)
            acc[:, cols] += jnp.dot(
                hidden[...], weights[tile, UNIT_TILE : 2 * UNIT_TILE, cols], preferred_element_type=F32
            )

    if split:
        at = 0
        for out, count in zip(outs, split):
            out[...] = acc[at : at + count, :].astype(BF16)
            at += count


def ffn(tokens, arrays, units, start=None, split=None, name="ffn"):
    copies, filled = unit_copies(units)
    tiles = filled // UNIT_TILE
    rows = tuple(token.shape[0] for token in tokens)
    total, width = sum(rows), tokens[0].shape[1]
    if split:
        out_shape = [jax.ShapeDtypeStruct((count, width), BF16) for count in split]
    else:
        out_shape = [jax.ShapeDtypeStruct((total, width), F32)]
    acc_rows = total if split else 8
    result = pl.pallas_call(
        functools.partial(ffn_kernel, rows, len(arrays), copies, start is not None, split),
        out_shape=out_shape,
        in_specs=[hbm()] * (len(tokens) + len(arrays) + (start is not None)),
        out_specs=[vmem()] * len(out_shape),
        scratch_shapes=[
            pltpu.VMEM((total, width), BF16),
            pltpu.VMEM((tiles, 2 * UNIT_TILE, width), BF16),
            pltpu.VMEM((total, UNIT_TILE), BF16),
            pltpu.VMEM((acc_rows, width), F32),
            pltpu.SemaphoreType.DMA((len(tokens),)),
            pltpu.SemaphoreType.DMA((tiles,)),
            pltpu.SemaphoreType.DMA,
        ],
        compiler_params=params(),
        cost_estimate=cost(4 * total * filled * width, 2 * total * width * 3 + 4 * filled * width),
        name=name,
    )(*tokens, *arrays, *(() if start is None else (start,)))
    return result if split else result[0]


def rows_of(value, start, count):
    return lax.dynamic_slice_in_dim(value, start, count, 0)


def body(residual, suffix_proj, prefix_cache, owner_req, lengths, norm_gain, up, down):
    width = residual.shape[3]
    me = lax.axis_index("req")
    group = lax.axis_index("grp")
    xl, y = me // 4, me % 4
    owner = lax.dynamic_index_in_dim(owner_req, group, 0, keepdims=False)
    slopes = jnp.exp2(-8.0 * jnp.arange(1, HEADS + 1, dtype=F32) / HEADS)

    dests = jnp.stack([((xl + dx) % 2) * 4 + (y + dy) % 4 for dx, dy in OFFSETS]).astype(jnp.int32)
    origins = jnp.stack([((xl + dx) % 2) * 4 + (y - dy) % 4 for dx, dy in OFFSETS]).astype(jnp.int32)
    cuts = cut_slices(dests, prefix_cache.reshape(256, width))
    kept = cuts[0]
    for place in range(1, 8):
        got = send(cuts[place], req_offset(*OFFSETS[place]))
        kept = jnp.where(origins[place] == owner, got, kept)
    pieces = [kept] + [send(kept, req_offset(*OFFSETS[place])) for place in range(1, 8)]

    other = (1 - xl) * 4 + y
    first = other * 64
    shard_send = jnp.concatenate(
        [rows_of(up, first, 32), rows_of(down, first, 32), rows_of(up, first + 32, 32), rows_of(down, first + 32, 32)]
    )
    shard = send(shard_send, X_CUT)
    direct_a = send(jnp.concatenate([up[512:640], down[512:640]]), X_CUT)
    direct_b = send(jnp.concatenate([up[640:768], down[640:768]]), X_CUT)

    suffix = suffix_part(slopes, suffix_proj[0, 0])
    states, normed = prefix_part(
        slopes, origins, suffix_proj[0, 0, 0], suffix, residual[0, 0], norm_gain, pieces
    )

    shard, _ = lax.optimization_barrier((shard, pieces))
    a_own, b_own = shard[:64], shard[64:]
    a_x = send(a_own, X_LOW)
    b_m, b_p = send(b_own, Y_UP), send(b_own, Y_DOWN)
    a_pair = jnp.concatenate([a_own, a_x])
    a_m, a_p = send(a_pair, Y_UP), send(a_pair, Y_DOWN)
    b_2u, b_2d = send(b_m[:32], Y_UP), send(b_p[32:], Y_DOWN)
    b_x = send(jnp.concatenate([b_own, b_m, b_p]), X_LOW)
    a_2u, a_2d = send(a_m[:64], Y_UP), send(a_p[64:], Y_DOWN)
    b_x2 = send(jnp.concatenate([b_2u, b_2d]), X_LOW)
    far = [shard, direct_a, direct_b, a_x, b_m, b_p, a_m, a_p, b_2u, b_2d, b_x, a_2u, a_2d, b_x2]
    far_units = [
        (0, 0, 0, 32, 32), (0, 64, 0, 96, 32), (1, 0, 1, 128, 128), (3, 0, 3, 32, 32),
        (4, 0, 4, 32, 32), (5, 0, 5, 32, 32), (6, 0, 6, 32, 32), (6, 64, 6, 96, 32),
        (7, 0, 7, 32, 32), (7, 64, 7, 96, 32), (8, 0, 9, 0, 32),
        (10, 0, 10, 32, 32), (10, 64, 10, 96, 32), (10, 128, 10, 160, 32),
        (11, 0, 11, 32, 32), (12, 0, 12, 32, 32), (13, 0, 13, 32, 32), (2, 0, 2, 128, 128),
    ]
    near, near_units = [up, down], [(0, 0, 1, 0, 768)]

    t_m, t_p = send(normed, Z_UP), send(normed, Z_DOWN)
    t_0c = send(normed, CORE)
    t_2u, t_2d = send(t_m[:64], Z_UP), send(t_p[64:], Z_DOWN)
    t_mc, t_pc = send(t_m, CORE), send(t_p, CORE)
    t_2uc, t_2dc = send(t_2u, CORE), send(t_2d, CORE)
    own = [normed, t_0c]
    side = [t_m, t_p, t_mc, t_pc]
    far_z = [t_2u, t_2d, t_2uc, t_2dc]
    y_own = ffn(own, near, near_units, name="near_own")
    y_side = ffn(side, near, near_units, name="near_side")
    y_far = ffn(far_z, near, near_units, name="near_far")
    far_mine, far_other = ffn(far_z, far, far_units, y_far, (128, 128), name="far_far")
    m_mine, p_mine, m_other, p_other = ffn(side, far, far_units, y_side, (128, 128, 128, 128), name="far_side")
    own_mine, own_other = ffn(own, far, far_units, y_own, (128, 128), name="far_own")

    def plus(*values):
        return functools.reduce(lambda a, b: a + b, [value.astype(F32) for value in values])

    far_sum = plus(far_mine, send(far_other, CORE)).astype(BF16)
    to_p, to_m = send(far_sum[:64], Z_UP), send(far_sum[64:], Z_DOWN)
    p_all = plus(p_mine, send(p_other, CORE))
    m_all = plus(m_mine, send(m_other, CORE))
    p_all = jnp.concatenate([p_all[:64] + to_p.astype(F32), p_all[64:]]).astype(BF16)
    m_all = jnp.concatenate([m_all[:64], m_all[64:] + to_m.astype(F32)]).astype(BF16)
    from_m, from_p = send(p_all, Z_UP), send(m_all, Z_DOWN)
    own_core = send(own_other, CORE)
    live = jnp.arange(128, dtype=jnp.int32) < lengths[0, 0]
    combined = plus(states, own_mine, own_core, from_m, from_p)
    return jnp.where(live[:, None], combined, 0.0).astype(BF16)[None, None]


def solution(mesh):
    placed = (
        P("req", "grp", None, None),
        P("req", "grp", None, None, None),
        P("req", "grp", None, None, None),
        P(),
        P("req", "grp"),
        P(),
        P("grp", None),
        P("grp", None),
    )
    return jax.shard_map(
        body, mesh=mesh, in_specs=placed, out_specs=P("req", "grp", None, None), check_vma=False
    )
```

```python
import functools
import math

import jax
import jax.numpy as jnp
from jax import lax
from jax.experimental import pallas as pl
from jax.experimental.pallas import tpu as pltpu
from jax.sharding import PartitionSpec as P


HEADS = 32
NORM_EPS = 1e-05
AXES = ("req", "grp")
F32, BF16 = jnp.float32, jnp.bfloat16
VMEM_LIMIT = 60 * 1024 * 1024


def pairs(move):
    table = []
    for r in range(8):
        for g in range(16):
            xl, y, z, xh, c = r // 4, r % 4, g // 4, (g // 2) % 2, g % 2
            a, b, d, e, f = move(xl, y, z, xh, c)
            table.append((r * 16 + g, (a * 4 + b % 4) * 16 + (d % 4) * 4 + e * 2 + f))
    return tuple(table)


Z_UP = pairs(lambda xl, y, z, xh, c: (xl, y, z + 1, xh, c))
Z_DOWN = pairs(lambda xl, y, z, xh, c: (xl, y, z - 1, xh, c))
Y_UP = pairs(lambda xl, y, z, xh, c: (xl, y + 1, z, xh, c))
Y_DOWN = pairs(lambda xl, y, z, xh, c: (xl, y - 1, z, xh, c))
X_LOW = pairs(lambda xl, y, z, xh, c: (1 - xl, y, z, xh, c))
X_CUT = pairs(lambda xl, y, z, xh, c: (1 - xl, y, z, 1 - xh, c))
CORE = pairs(lambda xl, y, z, xh, c: (xl, y, z, xh, 1 - c))


def req_offset(dx, dy):
    return pairs(lambda xl, y, z, xh, c: ((xl + dx) % 2, y + dy, z, xh, c))


OFFSETS = tuple((dx, dy) for dx in range(2) for dy in (0, 1, 3, 2))


def send(value, table):
    return lax.ppermute(value, AXES, table)


def vmem():
    return pl.BlockSpec(memory_space=pltpu.VMEM)


def smem():
    return pl.BlockSpec(memory_space=pltpu.SMEM)


def hbm():
    return pl.BlockSpec(memory_space=pl.ANY)


def params():
    return pltpu.CompilerParams(vmem_limit_bytes=VMEM_LIMIT)


def cost(flops, nbytes):
    return pl.CostEstimate(flops=int(flops), bytes_accessed=int(nbytes), transcendentals=0)


def cut_kernel(index_ref, cache_ref, *outs):
    for place, out in enumerate(outs):
        row = pl.multiple_of(index_ref[place] * 32, 32)
        out[...] = cache_ref[pl.ds(row, 32), :]


def cut_slices(index, cache):
    width = cache.shape[1]
    return pl.pallas_call(
        cut_kernel,
        out_shape=[jax.ShapeDtypeStruct((32, width), BF16)] * 8,
        in_specs=[smem(), vmem()],
        out_specs=[vmem()] * 8,
        compiler_params=params(),
        cost_estimate=cost(0, 4 * cache.size),
        name="cut_slices",
    )(index, cache)


GROUP = 8


def suffix_kernel(slope_ref, proj_ref, context_ref, max_ref, total_ref):
    step = pl.program_id(0)
    row = lax.broadcasted_iota(jnp.int32, (128, 128), 0)
    col = lax.broadcasted_iota(jnp.int32, (128, 128), 1)
    offset = (col - row).astype(F32)
    seen = col <= row
    tops, totals = jnp.zeros((128, 128), F32), jnp.zeros((128, 128), F32)
    for j in range(GROUP):
        part = slice(j * 128, (j + 1) * 128)
        scores = lax.dot_general(
            proj_ref[0, :, part], proj_ref[1, :, part], (((1,), (1,)), ((), ())), preferred_element_type=F32
        )
        scores = scores * (1.0 / math.sqrt(128)) + slope_ref[step * GROUP + j] * offset
        scores = jnp.where(seen, scores, -jnp.inf)
        top = jnp.max(scores, axis=1, keepdims=True)
        weights = jnp.exp(scores - top)
        total = jnp.sum(weights, axis=1, keepdims=True)
        context_ref[:, part] = jnp.dot(weights.astype(BF16), proj_ref[2, :, part], preferred_element_type=F32)
        tops = jnp.where(col == j, top, tops)
        totals = jnp.where(col == j, total, totals)
    max_ref[0] = tops
    total_ref[0] = totals


def suffix_part(slopes, proj):
    width = proj.shape[2]
    steps = HEADS // GROUP
    stats = jax.ShapeDtypeStruct((steps, 128, 128), F32)
    stats_spec = pl.BlockSpec((1, 128, 128), lambda i: (i, 0, 0))
    return pl.pallas_call(
        suffix_kernel,
        grid=(steps,),
        out_shape=[jax.ShapeDtypeStruct((128, width), F32), stats, stats],
        in_specs=[smem(), pl.BlockSpec((3, 128, width // steps), lambda i: (0, 0, i))],
        out_specs=[pl.BlockSpec((128, width // steps), lambda i: (0, i)), stats_spec, stats_spec],
        compiler_params=params(),
        cost_estimate=cost(4 * 128 * 128 * width, 5 * 128 * width * 2),
        name="suffix_part",
    )(slopes, proj)


def prefix_kernel(
    slope_ref, place_ref, query_ref, context_ref, max_ref, total_ref, residual_ref, gain_ref,
    s0, s1, s2, s3, s4, s5, s6, s7, state_ref, normed_ref, cached,
):
    for place, piece in enumerate((s0, s1, s2, s3, s4, s5, s6, s7)):
        start = pl.multiple_of(place_ref[place] * 32, 32)
        cached[pl.ds(start, 32), :] = piece[...]
    row = lax.broadcasted_iota(jnp.int32, (128, 128), 0)
    col = lax.broadcasted_iota(jnp.int32, (128, 128), 1)
    offset = (col - row - 128).astype(F32)

    def heads(i, running):
        for j in range(GROUP):
            h = i * GROUP + j
            part = pl.ds(pl.multiple_of(h * 128, 128), 128)
            scores = lax.dot_general(
                query_ref[0, :, part], cached[0:128, part], (((1,), (1,)), ((), ())), preferred_element_type=F32
            )
            scores = scores * (1.0 / math.sqrt(128)) + slope_ref[h] * offset
            top = jnp.max(scores, axis=1, keepdims=True)
            weights = jnp.exp(scores - top)
            total = jnp.sum(weights, axis=1, keepdims=True)
            context = jnp.dot(weights.astype(BF16), cached[128:256, part], preferred_element_type=F32)
            other, other_total = max_ref[i, :, j : j + 1], total_ref[i, :, j : j + 1]
            joint = jnp.maximum(top, other)
            first, second = jnp.exp(top - joint), jnp.exp(other - joint)
            share = 1.0 / (first * total + second * other_total)
            merged = (first * share) * context + (second * share) * context_ref[:, part]
            state = (residual_ref[:, part].astype(F32) + merged).astype(BF16)
            state_ref[:, part] = state
            running = running + state.astype(F32)
        return running

    sums = lax.fori_loop(0, HEADS // GROUP, heads, jnp.zeros((128, 128), F32))
    width = state_ref.shape[1]
    mean = jnp.sum(sums, axis=1, keepdims=True) * (1.0 / width)
    squares = jnp.zeros((128, 128), F32)
    for h in range(HEADS):
        part = slice(h * 128, (h + 1) * 128)
        center = state_ref[:, part].astype(F32) - mean
        squares = squares + center * center
    spread = lax.rsqrt(jnp.sum(squares, axis=1, keepdims=True) * (1.0 / width) + NORM_EPS)
    for h in range(HEADS):
        part = slice(h * 128, (h + 1) * 128)
        center = state_ref[:, part].astype(F32) - mean
        normed_ref[:, part] = (center * spread * gain_ref[:, part]).astype(BF16)


def prefix_part(slopes, places, query, suffix, residual, gain, pieces):
    width = query.shape[2]
    return pl.pallas_call(
        prefix_kernel,
        grid=(1,),
        out_shape=[jax.ShapeDtypeStruct((128, width), BF16)] * 2,
        in_specs=[smem(), smem(), pl.BlockSpec((1, 128, width), lambda i: (0, 0, 0))] + [vmem()] * 13,
        out_specs=[vmem()] * 2,
        scratch_shapes=[pltpu.VMEM((256, width), BF16)],
        compiler_params=params(),
        cost_estimate=cost(4 * 128 * 128 * width, 12 * 128 * width * 2),
        name="prefix_part",
    )(slopes, places, query, *suffix, residual, gain.reshape(1, width), *pieces)


UNIT_TILE = 256
COLUMN_TILE = 1024


def unit_copies(units):
    ups, downs, filled = [], [], 0
    for up_at, up_row, down_at, down_row, count in units:
        done = 0
        while done < count:
            take = min(count - done, UNIT_TILE - filled % UNIT_TILE)
            ups.append((up_at, up_row + done, take, filled))
            downs.append((down_at, down_row + done, take, filled))
            done += take
            filled += take
    return ups, downs, filled


def ffn_kernel(token_rows, source_count, ups, downs, with_acc, split, *refs):
    tokens = refs[: len(token_rows)]
    sources = refs[len(token_rows) : len(token_rows) + source_count]
    rest = refs[len(token_rows) + source_count :]
    start_ref = rest[0] if with_acc else None
    rest = rest[1:] if with_acc else rest
    out_count = len(split)
    outs = rest[:out_count]
    rows_buf, up_buf, down_buf, hidden, acc, result, token_sem, up_sem, down_sem, acc_sem, out_sem = rest[out_count:]
    _, width = rows_buf.shape
    at = 0
    moves = []
    for i, count in enumerate(token_rows):
        move = pltpu.make_async_copy(tokens[i], rows_buf.at[pl.ds(at, count), :], token_sem.at[i])
        move.start()
        moves.append(move)
        at += count
    for index, row, count, place in ups:
        pltpu.make_async_copy(
            sources[index].at[pl.ds(row, count), :], up_buf.at[pl.ds(place, count), :], up_sem.at[place // UNIT_TILE]
        ).start()
    for index, row, count, place in downs:
        pltpu.make_async_copy(
            sources[index].at[pl.ds(row, count), :], down_buf.at[pl.ds(place, count), :], down_sem
        ).start()
    if with_acc:
        begin = pltpu.make_async_copy(start_ref, acc, acc_sem)
        begin.start()
    for move in moves:
        move.wait()

    @pl.loop(0, up_buf.shape[0] // UNIT_TILE)
    def _(tile):
        part = pl.ds(pl.multiple_of(tile * UNIT_TILE, UNIT_TILE), UNIT_TILE)
        pltpu.make_async_copy(up_buf.at[part, :], up_buf.at[part, :], up_sem.at[tile]).wait()
        pre = lax.dot_general(
            rows_buf[...], up_buf[part, :], (((1,), (1,)), ((), ())), preferred_element_type=F32
        )
        hidden[:, part] = (0.5 * pre * (1.0 + lax.erf(pre * math.sqrt(0.5)))).astype(BF16)

    pltpu.make_async_copy(down_buf, down_buf, down_sem).wait()
    if with_acc:
        begin.wait()

    def stores(n):
        cols = pl.ds(pl.multiple_of(n * COLUMN_TILE, COLUMN_TILE), COLUMN_TILE)
        at = 0
        for i, count in enumerate(split):
            yield pltpu.make_async_copy(result.at[pl.ds(at, count), cols], outs[i].at[:, cols], out_sem.at[n, i])
            at += count

    @pl.loop(0, width // COLUMN_TILE)
    def _(n):
        cols = pl.ds(pl.multiple_of(n * COLUMN_TILE, COLUMN_TILE), COLUMN_TILE)
        value = jnp.dot(hidden[...], down_buf[:, cols], preferred_element_type=F32)
        if with_acc:
            value = value + acc[:, cols]
        result[:, cols] = value.astype(result.dtype)
        for copy in stores(n):
            copy.start()

    @pl.loop(0, width // COLUMN_TILE)
    def _(n):
        for copy in stores(n):
            copy.wait()


def ffn(tokens, arrays, units, start=None, split=None):
    ups, downs, filled = unit_copies(units)
    rows = tuple(token.shape[0] for token in tokens)
    total, width = sum(rows), tokens[0].shape[1]
    kind = BF16 if split else F32
    split = split or (total,)
    result = pl.pallas_call(
        functools.partial(ffn_kernel, rows, len(arrays), ups, downs, start is not None, split),
        out_shape=[jax.ShapeDtypeStruct((count, width), kind) for count in split],
        in_specs=[hbm()] * (len(tokens) + len(arrays) + (start is not None)),
        out_specs=[hbm()] * len(split),
        scratch_shapes=[
            pltpu.VMEM((total, width), BF16),
            pltpu.VMEM((filled, width), BF16),
            pltpu.VMEM((filled, width), BF16),
            pltpu.VMEM((total, filled), BF16),
            pltpu.VMEM((total if start is not None else 8, width), F32),
            pltpu.VMEM((total, width), kind),
            pltpu.SemaphoreType.DMA((len(tokens),)),
            pltpu.SemaphoreType.DMA((filled // UNIT_TILE,)),
            pltpu.SemaphoreType.DMA,
            pltpu.SemaphoreType.DMA,
            pltpu.SemaphoreType.DMA((width // COLUMN_TILE, len(split))),
        ],
        compiler_params=params(),
        cost_estimate=cost(4 * total * filled * width, 2 * total * width * 3 + 4 * filled * width),
    )(*tokens, *arrays, *(() if start is None else (start,)))
    return result if len(split) > 1 else result[0]


def rows_of(value, start, count):
    return lax.dynamic_slice_in_dim(value, start, count, 0)


def body(residual, suffix_proj, prefix_cache, owner_req, lengths, norm_gain, up, down):
    width = residual.shape[3]
    me = lax.axis_index("req")
    group = lax.axis_index("grp")
    xl, y = me // 4, me % 4
    owner = lax.dynamic_index_in_dim(owner_req, group, 0, keepdims=False)
    slopes = jnp.exp2(-8.0 * jnp.arange(1, HEADS + 1, dtype=F32) / HEADS)

    dests = jnp.stack([((xl + dx) % 2) * 4 + (y + dy) % 4 for dx, dy in OFFSETS]).astype(jnp.int32)
    origins = jnp.stack([((xl + dx) % 2) * 4 + (y - dy) % 4 for dx, dy in OFFSETS]).astype(jnp.int32)
    cuts = cut_slices(dests, prefix_cache.reshape(256, width))
    kept = cuts[0]
    for place in range(1, 8):
        got = send(cuts[place], req_offset(*OFFSETS[place]))
        kept = jnp.where(origins[place] == owner, got, kept)
    pieces = [kept] + [send(kept, req_offset(*OFFSETS[place])) for place in range(1, 8)]

    other = (1 - xl) * 4 + y
    first = other * 64
    shard_send = jnp.concatenate(
        [rows_of(up, first, 32), rows_of(down, first, 32), rows_of(up, first + 32, 32), rows_of(down, first + 32, 32)]
    )
    shard = send(shard_send, X_CUT)
    direct_a = send(jnp.concatenate([up[512:640], down[512:640]]), X_CUT)
    direct_b = send(jnp.concatenate([up[640:768], down[640:768]]), X_CUT)

    suffix = suffix_part(slopes, suffix_proj[0, 0])
    states, normed = prefix_part(
        slopes, origins, suffix_proj[0, 0], suffix, residual[0, 0], norm_gain, pieces
    )

    shard, _ = lax.optimization_barrier((shard, pieces))
    a_own, b_own = shard[:64], shard[64:]
    a_x = send(a_own, X_LOW)
    b_m, b_p = send(b_own, Y_UP), send(b_own, Y_DOWN)
    a_pair = jnp.concatenate([a_own, a_x])
    a_m, a_p = send(a_pair, Y_UP), send(a_pair, Y_DOWN)
    b_2u, b_2d = send(b_m[:32], Y_UP), send(b_p[32:], Y_DOWN)
    b_x = send(jnp.concatenate([b_own, b_m, b_p]), X_LOW)
    a_2u, a_2d = send(a_m[:64], Y_UP), send(a_p[64:], Y_DOWN)
    b_x2 = send(jnp.concatenate([b_2u, b_2d]), X_LOW)
    far = [shard, direct_a, direct_b, a_x, b_m, b_p, a_m, a_p, b_2u, b_2d, b_x, a_2u, a_2d, b_x2]
    far_units = [
        (0, 0, 0, 32, 32), (0, 64, 0, 96, 32), (1, 0, 1, 128, 128), (3, 0, 3, 32, 32),
        (4, 0, 4, 32, 32), (5, 0, 5, 32, 32), (6, 0, 6, 32, 32), (6, 64, 6, 96, 32),
        (7, 0, 7, 32, 32), (7, 64, 7, 96, 32), (8, 0, 9, 0, 32),
        (10, 0, 10, 32, 32), (10, 64, 10, 96, 32), (10, 128, 10, 160, 32),
        (11, 0, 11, 32, 32), (12, 0, 12, 32, 32), (13, 0, 13, 32, 32), (2, 0, 2, 128, 128),
    ]
    near, near_units = [up, down], [(0, 0, 1, 0, 768)]

    t_m, t_p = send(normed, Z_UP), send(normed, Z_DOWN)
    t_0c = send(normed, CORE)
    t_2u, t_2d = send(t_m[:64], Z_UP), send(t_p[64:], Z_DOWN)
    t_mc, t_pc = send(t_m, CORE), send(t_p, CORE)
    t_2uc, t_2dc = send(t_2u, CORE), send(t_2d, CORE)
    own = [normed, t_0c]
    side = [t_m, t_p, t_mc, t_pc]
    far_z = [t_2u, t_2d, t_2uc, t_2dc]
    y_own = ffn(own, near, near_units)
    y_side = ffn(side, near, near_units)
    y_far = ffn(far_z, near, near_units)
    far_mine, far_other = ffn(far_z, far, far_units, y_far, (128, 128))
    m_mine, p_mine, m_other, p_other = ffn(side, far, far_units, y_side, (128, 128, 128, 128))
    own_mine, own_other = ffn(own, far, far_units, y_own, (128, 128))

    def plus(*values):
        return functools.reduce(lambda a, b: a + b, [value.astype(F32) for value in values])

    far_sum = plus(far_mine, send(far_other, CORE)).astype(BF16)
    to_p, to_m = send(far_sum[:64], Z_UP), send(far_sum[64:], Z_DOWN)
    low, high = ((0, 64), (0, 0)), ((64, 0), (0, 0))
    p_all = plus(p_mine, send(p_other, CORE), jnp.pad(to_p, low)).astype(BF16)
    m_all = plus(m_mine, send(m_other, CORE), jnp.pad(to_m, high)).astype(BF16)
    from_m, from_p = send(p_all, Z_UP), send(m_all, Z_DOWN)
    own_core = send(own_other, CORE)
    live = jnp.arange(128, dtype=jnp.int32) < lengths[0, 0]
    combined = plus(states, own_mine, own_core, from_m, from_p)
    return jnp.where(live[:, None], combined, 0.0).astype(BF16)[None, None]


def solution(mesh):
    placed = (
        P("req", "grp", None, None),
        P("req", "grp", None, None, None),
        P("req", "grp", None, None, None),
        P(),
        P("req", "grp"),
        P(),
        P("grp", None),
        P("grp", None),
    )
    return jax.shard_map(body, mesh=mesh, in_specs=placed, out_specs=P("req", "grp", None, None), check_vma=False)
```

```python
import functools
import math

import jax
import jax.numpy as jnp
from jax import lax
from jax.experimental import pallas as pl
from jax.experimental.pallas import tpu as pltpu
from jax.sharding import PartitionSpec as P


HEADS = 32
NORM_EPS = 1e-05
AXES = ("req", "grp")
F32, BF16 = jnp.float32, jnp.bfloat16
VMEM_LIMIT = 60 * 1024 * 1024


def pairs(move):
    table = []
    for r in range(8):
        for g in range(16):
            xl, y, z, xh, c = r // 4, r % 4, g // 4, (g // 2) % 2, g % 2
            a, b, d, e, f = move(xl, y, z, xh, c)
            table.append((r * 16 + g, (a * 4 + b % 4) * 16 + (d % 4) * 4 + e * 2 + f))
    return tuple(table)


Z_UP = pairs(lambda xl, y, z, xh, c: (xl, y, z + 1, xh, c))
Z_DOWN = pairs(lambda xl, y, z, xh, c: (xl, y, z - 1, xh, c))
Y_UP = pairs(lambda xl, y, z, xh, c: (xl, y + 1, z, xh, c))
Y_DOWN = pairs(lambda xl, y, z, xh, c: (xl, y - 1, z, xh, c))
X_LOW = pairs(lambda xl, y, z, xh, c: (1 - xl, y, z, xh, c))
X_CUT = pairs(lambda xl, y, z, xh, c: (1 - xl, y, z, 1 - xh, c))
CORE = pairs(lambda xl, y, z, xh, c: (xl, y, z, xh, 1 - c))


def req_offset(dx, dy):
    return pairs(lambda xl, y, z, xh, c: ((xl + dx) % 2, y + dy, z, xh, c))


OFFSETS = tuple((dx, dy) for dx in range(2) for dy in (0, 1, 3, 2))


def send(value, table):
    return lax.ppermute(value, AXES, table)


def vmem():
    return pl.BlockSpec(memory_space=pltpu.VMEM)


def smem():
    return pl.BlockSpec(memory_space=pltpu.SMEM)


def hbm():
    return pl.BlockSpec(memory_space=pl.ANY)


def params():
    return pltpu.CompilerParams(vmem_limit_bytes=VMEM_LIMIT)


def cost(flops, nbytes):
    return pl.CostEstimate(flops=int(flops), bytes_accessed=int(nbytes), transcendentals=0)


def cut_kernel(index_ref, cache_ref, up_ref, down_ref, *refs):
    outs, share, sems = refs[:16], refs[16], refs[17]
    first = pl.multiple_of(index_ref[8] * 64, 64)
    moves = []
    for i, (source, row) in enumerate(((up_ref, 0), (down_ref, 0), (up_ref, 32), (down_ref, 32))):
        part = pl.ds(pl.multiple_of(first + row, 32), 32)
        moves.append(pltpu.make_async_copy(source.at[part, :], share.at[pl.ds(i * 32, 32), :], sems.at[i]))
    for move in moves:
        move.start()
    for place in range(8):
        row = pl.multiple_of(index_ref[place] * 16, 16)
        outs[place][...] = cache_ref[pl.ds(row, 16), :]
        outs[8 + place][...] = cache_ref[pl.ds(pl.multiple_of(128 + row, 16), 16), :]
    for move in moves:
        move.wait()


def cut_slices(index, cache, up, down):
    width = cache.shape[1]
    return pl.pallas_call(
        cut_kernel,
        out_shape=[jax.ShapeDtypeStruct((16, width), BF16)] * 16 + [jax.ShapeDtypeStruct((128, width), BF16)],
        in_specs=[smem(), vmem(), hbm(), hbm()],
        out_specs=[vmem()] * 17,
        scratch_shapes=[pltpu.SemaphoreType.DMA((4,))],
        compiler_params=params(),
        cost_estimate=cost(0, 6 * cache.size),
        name="cut_slices",
    )(index, cache, up, down)


def direct_kernel(up_ref, down_ref, out_ref, sems):
    moves = [
        pltpu.make_async_copy(up_ref.at[pl.ds(512, 256), :], out_ref.at[pl.ds(0, 256), :], sems.at[0]),
        pltpu.make_async_copy(down_ref.at[pl.ds(512, 256), :], out_ref.at[pl.ds(256, 256), :], sems.at[1]),
    ]
    for move in moves:
        move.start()
    for move in moves:
        move.wait()


def direct_rows(up, down):
    width = up.shape[1]
    return pl.pallas_call(
        direct_kernel,
        out_shape=jax.ShapeDtypeStruct((512, width), BF16),
        in_specs=[hbm(), hbm()],
        out_specs=vmem(),
        scratch_shapes=[pltpu.SemaphoreType.DMA((2,))],
        compiler_params=params(),
        cost_estimate=cost(0, 4 * 512 * width),
        name="direct_rows",
    )(up, down)


GROUP = 8


def attention_kernel(slope_ref, place_ref, proj_ref, residual_ref, gain_ref, *refs):
    pieces, (state_ref, normed_ref, keys, values, bias, sums) = refs[:16], refs[16:]
    for place in range(8):
        start = pl.multiple_of(place_ref[place] * 16, 16)
        keys[pl.ds(start, 16), :] = pieces[place][...]
        values[pl.ds(start, 16), :] = pieces[8 + place][...]
    row = lax.broadcasted_iota(jnp.int32, (128, 256), 0)
    col = lax.broadcasted_iota(jnp.int32, (128, 256), 1)
    bias[...] = jnp.where(col - 128 <= row, (col - 128 - row).astype(F32), -1e30)
    sums[...] = jnp.zeros((128, 128), F32)
    ones = jnp.ones((256, 128), BF16)

    @pl.loop(0, HEADS // GROUP)
    def _(i):
        for j in range(GROUP):
            h = i * GROUP + j
            part = pl.ds(pl.multiple_of(h * 128, 128), 128)
            key = jnp.concatenate([keys[:, part], proj_ref[1, :, part]], axis=0)
            value = jnp.concatenate([values[:, part], proj_ref[2, :, part]], axis=0)
            value = jnp.concatenate([value, ones], axis=1)
            scores = lax.dot_general(
                proj_ref[0, :, part], key, (((1,), (1,)), ((), ())), preferred_element_type=F32
            )
            scores = scores * (1.0 / math.sqrt(128)) + slope_ref[h] * bias[...]
            top = jnp.max(jnp.maximum(scores[:, :128], scores[:, 128:]), axis=1, keepdims=True)
            weights = jnp.exp(scores - top).astype(BF16)
            both = jnp.dot(weights, value, preferred_element_type=F32)
            state = (residual_ref[:, part].astype(F32) + both[:, :128] / both[:, 128:]).astype(BF16)
            state_ref[:, part] = state
            sums[...] += state.astype(F32)

    width = state_ref.shape[1]
    mean = jnp.broadcast_to(jnp.sum(sums[...], axis=1, keepdims=True) * (1.0 / width), (128, 128))
    squares = jnp.zeros((128, 128), F32)
    for h in range(HEADS):
        part = slice(h * 128, (h + 1) * 128)
        center = state_ref[:, part].astype(F32) - mean
        squares = squares + center * center
    spread = lax.rsqrt(jnp.sum(squares, axis=1, keepdims=True) * (1.0 / width) + NORM_EPS)
    spread = jnp.broadcast_to(spread, (128, 128))
    for h in range(HEADS):
        part = slice(h * 128, (h + 1) * 128)
        center = state_ref[:, part].astype(F32) - mean
        normed_ref[:, part] = (center * spread * gain_ref[:, part]).astype(BF16)


def attention(slopes, places, proj, residual, gain, pieces):
    width = proj.shape[2]
    return pl.pallas_call(
        attention_kernel,
        out_shape=[jax.ShapeDtypeStruct((128, width), BF16)] * 2,
        in_specs=[smem(), smem()] + [vmem()] * 19,
        out_specs=[vmem()] * 2,
        scratch_shapes=[pltpu.VMEM((128, width), BF16)] * 2
        + [pltpu.VMEM((128, 256), F32), pltpu.VMEM((128, 128), F32)],
        compiler_params=params(),
        cost_estimate=cost(8 * 128 * 256 * width, 8 * 128 * width * 2),
        name="attention",
    )(slopes, places, proj, residual, gain.reshape(1, width), *pieces)


UNIT_TILE = 256
COLUMN_TILE = 1024


def unit_copies(units):
    ups, downs, filled = [], [], 0
    for up_at, up_row, down_at, down_row, count in units:
        done = 0
        while done < count:
            take = min(count - done, UNIT_TILE - filled % UNIT_TILE)
            ups.append((up_at, up_row + done, take, filled))
            downs.append((down_at, down_row + done, take, filled))
            done += take
            filled += take
    return ups, downs, filled


def ffn_kernel(token_rows, source_count, ups, downs, with_acc, split, *refs):
    tokens = refs[: len(token_rows)]
    sources = refs[len(token_rows) : len(token_rows) + source_count]
    rest = refs[len(token_rows) + source_count :]
    start_ref = rest[0] if with_acc else None
    rest = rest[1:] if with_acc else rest
    out_count = len(split)
    outs = rest[:out_count]
    rows_buf, up_buf, down_buf, hidden, acc, result, token_sem, up_sem, down_sem, acc_sem, out_sem = rest[out_count:]
    _, width = rows_buf.shape
    at = 0
    moves = []
    for i, count in enumerate(token_rows):
        move = pltpu.make_async_copy(tokens[i], rows_buf.at[pl.ds(at, count), :], token_sem.at[i])
        move.start()
        moves.append(move)
        at += count
    for index, row, count, place in ups:
        pltpu.make_async_copy(
            sources[index].at[pl.ds(row, count), :], up_buf.at[pl.ds(place, count), :], up_sem.at[place // UNIT_TILE]
        ).start()
    for index, row, count, place in downs:
        pltpu.make_async_copy(
            sources[index].at[pl.ds(row, count), :], down_buf.at[pl.ds(place, count), :], down_sem
        ).start()
    if with_acc:
        begin = pltpu.make_async_copy(start_ref, acc, acc_sem)
        begin.start()
    for move in moves:
        move.wait()

    @pl.loop(0, up_buf.shape[0] // UNIT_TILE)
    def _(tile):
        part = pl.ds(pl.multiple_of(tile * UNIT_TILE, UNIT_TILE), UNIT_TILE)
        pltpu.make_async_copy(up_buf.at[part, :], up_buf.at[part, :], up_sem.at[tile]).wait()
        pre = lax.dot_general(
            rows_buf[...], up_buf[part, :], (((1,), (1,)), ((), ())), preferred_element_type=F32
        )
        hidden[:, part] = (0.5 * pre * (1.0 + lax.erf(pre * math.sqrt(0.5)))).astype(BF16)

    pltpu.make_async_copy(down_buf, down_buf, down_sem).wait()
    if with_acc:
        begin.wait()

    def stores(n):
        cols = pl.ds(pl.multiple_of(n * COLUMN_TILE, COLUMN_TILE), COLUMN_TILE)
        at = 0
        for i, count in enumerate(split):
            yield pltpu.make_async_copy(result.at[pl.ds(at, count), cols], outs[i].at[:, cols], out_sem.at[n, i])
            at += count

    @pl.loop(0, width // COLUMN_TILE)
    def _(n):
        cols = pl.ds(pl.multiple_of(n * COLUMN_TILE, COLUMN_TILE), COLUMN_TILE)
        value = jnp.dot(hidden[...], down_buf[:, cols], preferred_element_type=F32)
        if with_acc:
            value = value + acc[:, cols]
        result[:, cols] = value.astype(result.dtype)
        for copy in stores(n):
            copy.start()

    @pl.loop(0, width // COLUMN_TILE)
    def _(n):
        for copy in stores(n):
            copy.wait()


def ffn(tokens, arrays, units, start=None, split=None):
    ups, downs, filled = unit_copies(units)
    rows = tuple(token.shape[0] for token in tokens)
    total, width = sum(rows), tokens[0].shape[1]
    kind = BF16 if split else F32
    split = split or (total,)
    result = pl.pallas_call(
        functools.partial(ffn_kernel, rows, len(arrays), ups, downs, start is not None, split),
        out_shape=[jax.ShapeDtypeStruct((count, width), kind) for count in split],
        in_specs=[hbm()] * (len(tokens) + len(arrays) + (start is not None)),
        out_specs=[hbm()] * len(split),
        scratch_shapes=[
            pltpu.VMEM((total, width), BF16),
            pltpu.VMEM((filled, width), BF16),
            pltpu.VMEM((filled, width), BF16),
            pltpu.VMEM((total, filled), BF16),
            pltpu.VMEM((total if start is not None else 8, width), F32),
            pltpu.VMEM((total, width), kind),
            pltpu.SemaphoreType.DMA((len(tokens),)),
            pltpu.SemaphoreType.DMA((filled // UNIT_TILE,)),
            pltpu.SemaphoreType.DMA,
            pltpu.SemaphoreType.DMA,
            pltpu.SemaphoreType.DMA((width // COLUMN_TILE, len(split))),
        ],
        compiler_params=params(),
        cost_estimate=cost(4 * total * filled * width, 2 * total * width * 3 + 4 * filled * width),
    )(*tokens, *arrays, *(() if start is None else (start,)))
    return result if len(split) > 1 else result[0]


def body(residual, suffix_proj, prefix_cache, owner_req, lengths, norm_gain, up, down):
    width = residual.shape[3]
    me = lax.axis_index("req")
    group = lax.axis_index("grp")
    xl, y = me // 4, me % 4
    owner = lax.dynamic_index_in_dim(owner_req, group, 0, keepdims=False)
    slopes = jnp.exp2(-8.0 * jnp.arange(1, HEADS + 1, dtype=F32) / HEADS)

    other = (1 - xl) * 4 + y
    dests = [((xl + dx) % 2) * 4 + (y + dy) % 4 for dx, dy in OFFSETS]
    origins = jnp.stack([((xl + dx) % 2) * 4 + (y - dy) % 4 for dx, dy in OFFSETS]).astype(jnp.int32)
    cuts = cut_slices(jnp.stack(dests + [other]).astype(jnp.int32), prefix_cache.reshape(256, width), up, down)
    pieces = []
    for part in (cuts[:8], cuts[8:16]):
        kept = part[0]
        for place in range(1, 8):
            got = send(part[place], req_offset(*OFFSETS[place]))
            kept = jnp.where(origins[place] == owner, got, kept)
        pieces += [kept] + [send(kept, req_offset(*OFFSETS[place])) for place in range(1, 8)]

    shard = send(cuts[16], X_CUT)
    direct = send(direct_rows(up, down), X_CUT)

    states, normed = attention(slopes, origins, suffix_proj[0, 0], residual[0, 0], norm_gain, pieces)

    shard, _ = lax.optimization_barrier((shard, pieces))
    a_own, b_own = shard[:64], shard[64:]
    a_x = send(a_own, X_LOW)
    b_m, b_p = send(b_own, Y_UP), send(b_own, Y_DOWN)
    a_pair = jnp.concatenate([a_own, a_x])
    a_m, a_p = send(a_pair, Y_UP), send(a_pair, Y_DOWN)
    b_2u, b_2d = send(b_m[:32], Y_UP), send(b_p[32:], Y_DOWN)
    b_x = send(jnp.concatenate([b_own, b_m, b_p]), X_LOW)
    a_2u, a_2d = send(a_m[:64], Y_UP), send(a_p[64:], Y_DOWN)
    b_x2 = send(jnp.concatenate([b_2u, b_2d]), X_LOW)
    far = [shard, direct, a_x, b_m, b_p, a_m, a_p, b_2u, b_2d, b_x, a_2u, a_2d, b_x2]
    far_units = [
        (0, 0, 0, 32, 32), (0, 64, 0, 96, 32), (1, 0, 1, 256, 256), (2, 0, 2, 32, 32),
        (3, 0, 3, 32, 32), (4, 0, 4, 32, 32), (5, 0, 5, 32, 32), (5, 64, 5, 96, 32),
        (6, 0, 6, 32, 32), (6, 64, 6, 96, 32), (7, 0, 8, 0, 32),
        (9, 0, 9, 32, 32), (9, 64, 9, 96, 32), (9, 128, 9, 160, 32),
        (10, 0, 10, 32, 32), (11, 0, 11, 32, 32), (12, 0, 12, 32, 32),
    ]
    near, near_units = [up, down], [(0, 0, 1, 0, 768)]

    t_m, t_p = send(normed, Z_UP), send(normed, Z_DOWN)
    t_0c = send(normed, CORE)
    t_2u, t_2d = send(t_m[:64], Z_UP), send(t_p[64:], Z_DOWN)
    t_mc, t_pc = send(t_m, CORE), send(t_p, CORE)
    t_2uc, t_2dc = send(t_2u, CORE), send(t_2d, CORE)
    own = [normed, t_0c]
    side = [t_m, t_p, t_mc, t_pc]
    far_z = [t_2u, t_2d, t_2uc, t_2dc]
    y_own = ffn(own, near, near_units)
    y_side = ffn(side, near, near_units)
    y_far = ffn(far_z, near, near_units)
    far_mine, far_other = ffn(far_z, far, far_units, y_far, (128, 128))
    m_mine, p_mine, m_other, p_other = ffn(side, far, far_units, y_side, (128, 128, 128, 128))
    own_mine, own_other = ffn(own, far, far_units, y_own, (128, 128))

    def plus(*values):
        return functools.reduce(lambda a, b: a + b, [value.astype(F32) for value in values])

    far_sum = plus(far_mine, send(far_other, CORE)).astype(BF16)
    to_p, to_m = send(far_sum[:64], Z_UP), send(far_sum[64:], Z_DOWN)
    low, high = ((0, 64), (0, 0)), ((64, 0), (0, 0))
    p_all = plus(p_mine, send(p_other, CORE), jnp.pad(to_p, low)).astype(BF16)
    m_all = plus(m_mine, send(m_other, CORE), jnp.pad(to_m, high)).astype(BF16)
    from_m, from_p = send(p_all, Z_UP), send(m_all, Z_DOWN)
    own_core = send(own_other, CORE)
    live = jnp.arange(128, dtype=jnp.int32) < lengths[0, 0]
    combined = plus(states, own_mine, own_core, from_m, from_p)
    return jnp.where(live[:, None], combined, 0.0).astype(BF16)[None, None]


def solution(mesh):
    placed = (
        P("req", "grp", None, None),
        P("req", "grp", None, None, None),
        P("req", "grp", None, None, None),
        P(),
        P("req", "grp"),
        P(),
        P("grp", None),
        P("grp", None),
    )
    return jax.shard_map(body, mesh=mesh, in_specs=placed, out_specs=P("req", "grp", None, None), check_vma=False)
```

```python
import functools
import math

import jax
import jax.numpy as jnp
from jax import lax
from jax.experimental import pallas as pl
from jax.experimental.pallas import tpu as pltpu
from jax.sharding import PartitionSpec as P


HEADS = 32
NORM_EPS = 1e-05
AXES = ("req", "grp")
F32, BF16 = jnp.float32, jnp.bfloat16
VMEM_LIMIT = 60 * 1024 * 1024


def pairs(move):
    table = []
    for r in range(8):
        for g in range(16):
            xl, y, z, xh, c = r // 4, r % 4, g // 4, (g // 2) % 2, g % 2
            a, b, d, e, f = move(xl, y, z, xh, c)
            table.append((r * 16 + g, (a * 4 + b % 4) * 16 + (d % 4) * 4 + e * 2 + f))
    return tuple(table)


Z_UP = pairs(lambda xl, y, z, xh, c: (xl, y, z + 1, xh, c))
Z_DOWN = pairs(lambda xl, y, z, xh, c: (xl, y, z - 1, xh, c))
Y_UP = pairs(lambda xl, y, z, xh, c: (xl, y + 1, z, xh, c))
Y_DOWN = pairs(lambda xl, y, z, xh, c: (xl, y - 1, z, xh, c))
X_LOW = pairs(lambda xl, y, z, xh, c: (1 - xl, y, z, xh, c))
X_CUT = pairs(lambda xl, y, z, xh, c: (1 - xl, y, z, 1 - xh, c))
CORE = pairs(lambda xl, y, z, xh, c: (xl, y, z, xh, 1 - c))


def req_offset(dx, dy):
    return pairs(lambda xl, y, z, xh, c: ((xl + dx) % 2, y + dy, z, xh, c))


OFFSETS = ((0, 0), (1, 2), (0, 2), (1, 1), (1, 3), (0, 1), (0, 3), (1, 0))


def send(value, table):
    return lax.ppermute(value, AXES, table)


def vmem():
    return pl.BlockSpec(memory_space=pltpu.VMEM)


def smem():
    return pl.BlockSpec(memory_space=pltpu.SMEM)


def hbm():
    return pl.BlockSpec(memory_space=pl.ANY)


def params():
    return pltpu.CompilerParams(vmem_limit_bytes=VMEM_LIMIT)


def cost(flops, nbytes):
    return pl.CostEstimate(flops=int(flops), bytes_accessed=int(nbytes), transcendentals=0)


def cut_kernel(index_ref, cache_ref, up_ref, down_ref, *refs):
    outs, share, sems = refs[:8], refs[8], refs[9]
    first = pl.multiple_of(index_ref[8] * 64, 64)
    moves = []
    for i, (source, row) in enumerate(((up_ref, 0), (down_ref, 0), (up_ref, 32), (down_ref, 32))):
        part = pl.ds(pl.multiple_of(first + row, 32), 32)
        moves.append(pltpu.make_async_copy(source.at[part, :], share.at[pl.ds(i * 32, 32), :], sems.at[i]))
    for move in moves:
        move.start()
    for place in range(8):
        row = pl.multiple_of(index_ref[place] * 32, 32)
        outs[place][...] = cache_ref[pl.ds(row, 32), :]
    for move in moves:
        move.wait()


def cut_slices(index, cache, up, down):
    width = cache.shape[1]
    return pl.pallas_call(
        cut_kernel,
        out_shape=[jax.ShapeDtypeStruct((32, width), BF16)] * 8 + [jax.ShapeDtypeStruct((128, width), BF16)],
        in_specs=[smem(), vmem(), hbm(), hbm()],
        out_specs=[vmem()] * 9,
        scratch_shapes=[pltpu.SemaphoreType.DMA((4,))],
        compiler_params=params(),
        cost_estimate=cost(0, 6 * cache.size),
        name="cut_slices",
    )(index, cache, up, down)


def direct_kernel(up_ref, down_ref, out_ref, sems):
    moves = [
        pltpu.make_async_copy(up_ref.at[pl.ds(512, 256), :], out_ref.at[pl.ds(0, 256), :], sems.at[0]),
        pltpu.make_async_copy(down_ref.at[pl.ds(512, 256), :], out_ref.at[pl.ds(256, 256), :], sems.at[1]),
    ]
    for move in moves:
        move.start()
    for move in moves:
        move.wait()


def direct_rows(up, down):
    width = up.shape[1]
    return pl.pallas_call(
        direct_kernel,
        out_shape=jax.ShapeDtypeStruct((512, width), BF16),
        in_specs=[hbm(), hbm()],
        out_specs=vmem(),
        scratch_shapes=[pltpu.SemaphoreType.DMA((2,))],
        compiler_params=params(),
        cost_estimate=cost(0, 4 * 512 * width),
        name="direct_rows",
    )(up, down)


GROUP = 8


def attention_kernel(slope_ref, place_ref, proj_ref, residual_ref, gain_ref, *refs):
    pieces, (state_ref, low_ref, high_ref, cached, bias, sums) = refs[:8], refs[8:]
    for place in range(8):
        cached[pl.ds(pl.multiple_of(place_ref[place] * 32, 32), 32), :] = pieces[place][...]
    row = lax.broadcasted_iota(jnp.int32, (128, 256), 0)
    col = lax.broadcasted_iota(jnp.int32, (128, 256), 1)
    bias[...] = jnp.where(col - 128 <= row, (col - 128 - row).astype(F32), -1e30)
    sums[...] = jnp.zeros((128, 128), F32)
    ones = jnp.ones((256, 128), BF16)

    @pl.loop(0, HEADS // GROUP)
    def _(i):
        for j in range(GROUP):
            h = i * GROUP + j
            part = pl.ds(pl.multiple_of(h * 128, 128), 128)
            key = jnp.concatenate([cached[0:128, part], proj_ref[1, :, part]], axis=0)
            value = jnp.concatenate([cached[128:256, part], proj_ref[2, :, part]], axis=0)
            value = jnp.concatenate([value, ones], axis=1)
            scores = lax.dot_general(
                proj_ref[0, :, part], key, (((1,), (1,)), ((), ())), preferred_element_type=F32
            )
            scores = scores * (1.0 / math.sqrt(128)) + slope_ref[h] * bias[...]
            top = jnp.max(jnp.maximum(scores[:, :128], scores[:, 128:]), axis=1, keepdims=True)
            weights = jnp.exp(scores - top).astype(BF16)
            both = jnp.dot(weights, value, preferred_element_type=F32)
            state = (residual_ref[:, part].astype(F32) + both[:, :128] / both[:, 128:]).astype(BF16)
            state_ref[:, part] = state
            sums[...] += state.astype(F32)

    width = state_ref.shape[1]
    mean = jnp.broadcast_to(jnp.sum(sums[...], axis=1, keepdims=True) * (1.0 / width), (128, 128))
    squares = jnp.zeros((128, 128), F32)
    for h in range(HEADS):
        part = slice(h * 128, (h + 1) * 128)
        center = state_ref[:, part].astype(F32) - mean
        squares = squares + center * center
    spread = lax.rsqrt(jnp.sum(squares, axis=1, keepdims=True) * (1.0 / width) + NORM_EPS)
    spread = jnp.broadcast_to(spread, (128, 128))
    for h in range(HEADS):
        part = slice(h * 128, (h + 1) * 128)
        center = state_ref[:, part].astype(F32) - mean
        normed = (center * spread * gain_ref[:, part]).astype(BF16)
        low_ref[:, part] = normed[:64]
        high_ref[:, part] = normed[64:]


def attention(slopes, places, proj, residual, gain, pieces):
    width = proj.shape[2]
    return pl.pallas_call(
        attention_kernel,
        out_shape=[jax.ShapeDtypeStruct((128, width), BF16)] + [jax.ShapeDtypeStruct((64, width), BF16)] * 2,
        in_specs=[smem(), smem()] + [vmem()] * 11,
        out_specs=[vmem()] * 3,
        scratch_shapes=[pltpu.VMEM((256, width), BF16)]
        + [pltpu.VMEM((128, 256), F32), pltpu.VMEM((128, 128), F32)],
        compiler_params=params(),
        cost_estimate=cost(8 * 128 * 256 * width, 8 * 128 * width * 2),
        name="attention",
    )(slopes, places, proj, residual, gain.reshape(1, width), *pieces)


UNIT_TILE = 256
COLUMN_TILE = 1024


def unit_copies(units):
    ups, downs, filled = [], [], 0
    for up_at, up_row, down_at, down_row, count in units:
        done = 0
        while done < count:
            take = min(count - done, UNIT_TILE - filled % UNIT_TILE)
            ups.append((up_at, up_row + done, take, filled))
            downs.append((down_at, down_row + done, take, filled))
            done += take
            filled += take
    return ups, downs, filled


def ffn_kernel(token_rows, source_count, ups, downs, with_acc, split, *refs):
    tokens = refs[: len(token_rows)]
    sources = refs[len(token_rows) : len(token_rows) + source_count]
    rest = refs[len(token_rows) + source_count :]
    start_ref = rest[0] if with_acc else None
    rest = rest[1:] if with_acc else rest
    out_count = len(split)
    outs = rest[:out_count]
    rows_buf, up_buf, down_buf, hidden, acc, result, token_sem, up_sem, down_sem, acc_sem, out_sem = rest[out_count:]
    _, width = rows_buf.shape
    at = 0
    moves = []
    for i, count in enumerate(token_rows):
        move = pltpu.make_async_copy(tokens[i], rows_buf.at[pl.ds(at, count), :], token_sem.at[i])
        move.start()
        moves.append(move)
        at += count
    for index, row, count, place in ups:
        pltpu.make_async_copy(
            sources[index].at[pl.ds(row, count), :], up_buf.at[pl.ds(place, count), :], up_sem.at[place // UNIT_TILE]
        ).start()
    for index, row, count, place in downs:
        pltpu.make_async_copy(
            sources[index].at[pl.ds(row, count), :], down_buf.at[pl.ds(place, count), :], down_sem
        ).start()
    if with_acc:
        begin = pltpu.make_async_copy(start_ref, acc, acc_sem)
        begin.start()
    for move in moves:
        move.wait()

    @pl.loop(0, up_buf.shape[0] // UNIT_TILE)
    def _(tile):
        part = pl.ds(pl.multiple_of(tile * UNIT_TILE, UNIT_TILE), UNIT_TILE)
        pltpu.make_async_copy(up_buf.at[part, :], up_buf.at[part, :], up_sem.at[tile]).wait()
        pre = lax.dot_general(
            rows_buf[...], up_buf[part, :], (((1,), (1,)), ((), ())), preferred_element_type=F32
        )
        hidden[:, part] = (0.5 * pre * (1.0 + lax.erf(pre * math.sqrt(0.5)))).astype(BF16)

    pltpu.make_async_copy(down_buf, down_buf, down_sem).wait()
    if with_acc:
        begin.wait()

    def stores(n):
        cols = pl.ds(pl.multiple_of(n * COLUMN_TILE, COLUMN_TILE), COLUMN_TILE)
        at = 0
        for i, count in enumerate(split):
            yield pltpu.make_async_copy(result.at[pl.ds(at, count), cols], outs[i].at[:, cols], out_sem.at[n, i])
            at += count

    @pl.loop(0, width // COLUMN_TILE)
    def _(n):
        cols = pl.ds(pl.multiple_of(n * COLUMN_TILE, COLUMN_TILE), COLUMN_TILE)
        value = jnp.dot(hidden[...], down_buf[:, cols], preferred_element_type=F32)
        if with_acc:
            value = value + acc[:, cols]
        result[:, cols] = value.astype(result.dtype)
        for copy in stores(n):
            copy.start()

    @pl.loop(0, width // COLUMN_TILE)
    def _(n):
        for copy in stores(n):
            copy.wait()


def ffn(tokens, arrays, units, start=None, split=None):
    ups, downs, filled = unit_copies(units)
    rows = tuple(token.shape[0] for token in tokens)
    total, width = sum(rows), tokens[0].shape[1]
    kind = BF16 if split else F32
    split = split or (total,)
    result = pl.pallas_call(
        functools.partial(ffn_kernel, rows, len(arrays), ups, downs, start is not None, split),
        out_shape=[jax.ShapeDtypeStruct((count, width), kind) for count in split],
        in_specs=[hbm()] * (len(tokens) + len(arrays) + (start is not None)),
        out_specs=[hbm()] * len(split),
        scratch_shapes=[
            pltpu.VMEM((total, width), BF16),
            pltpu.VMEM((filled, width), BF16),
            pltpu.VMEM((filled, width), BF16),
            pltpu.VMEM((total, filled), BF16),
            pltpu.VMEM((total if start is not None else 8, width), F32),
            pltpu.VMEM((total, width), kind),
            pltpu.SemaphoreType.DMA((len(tokens),)),
            pltpu.SemaphoreType.DMA((filled // UNIT_TILE,)),
            pltpu.SemaphoreType.DMA,
            pltpu.SemaphoreType.DMA,
            pltpu.SemaphoreType.DMA((width // COLUMN_TILE, len(split))),
        ],
        compiler_params=params(),
        cost_estimate=cost(4 * total * filled * width, 2 * total * width * 3 + 4 * filled * width),
    )(*tokens, *arrays, *(() if start is None else (start,)))
    return result if len(split) > 1 else result[0]


def body(residual, suffix_proj, prefix_cache, owner_req, lengths, norm_gain, up, down):
    width = residual.shape[3]
    me = lax.axis_index("req")
    group = lax.axis_index("grp")
    xl, y = me // 4, me % 4
    owner = lax.dynamic_index_in_dim(owner_req, group, 0, keepdims=False)
    slopes = jnp.exp2(-8.0 * jnp.arange(1, HEADS + 1, dtype=F32) / HEADS)

    other = (1 - xl) * 4 + y
    dests = [((xl + dx) % 2) * 4 + (y + dy) % 4 for dx, dy in OFFSETS]
    origins = jnp.stack([((xl + dx) % 2) * 4 + (y - dy) % 4 for dx, dy in OFFSETS]).astype(jnp.int32)
    cuts = cut_slices(jnp.stack(dests + [other]).astype(jnp.int32), prefix_cache.reshape(256, width), up, down)
    kept = cuts[0]
    for place in range(1, 8):
        got = send(cuts[place], req_offset(*OFFSETS[place]))
        kept = jnp.where(origins[place] == owner, got, kept)
    pieces = [kept] + [send(kept, req_offset(*OFFSETS[place])) for place in range(1, 8)]

    shard = send(cuts[8], X_CUT)
    direct = send(direct_rows(up, down), X_CUT)

    states, low, high = attention(slopes, origins, suffix_proj[0, 0], residual[0, 0], norm_gain, pieces)

    shard, _ = lax.optimization_barrier((shard, (pieces[5], pieces[6], pieces[7])))
    a_own, b_own = shard[:64], shard[64:]
    a_x = send(a_own, X_LOW)
    b_m, b_p = send(b_own, Y_UP), send(b_own, Y_DOWN)
    b_2 = send(b_own, req_offset(0, 2))
    b_x = send(jnp.concatenate([b_own, b_m, b_p, b_2]), X_LOW)
    a_pair = jnp.concatenate([a_own, a_x])
    a_m, a_p = send(a_pair, Y_UP), send(a_pair, Y_DOWN)
    a_2 = send(a_pair, req_offset(0, 2))
    far = [shard, direct, a_x, b_m, b_p, b_2, b_x, a_m, a_p, a_2]
    pieces_of = lambda index, count: [(index, 64 * i, index, 64 * i + 32, 32) for i in range(count)]
    far_units = [
        *pieces_of(0, 2), (1, 0, 1, 256, 256), *pieces_of(2, 1), *pieces_of(3, 1), *pieces_of(4, 1), *pieces_of(5, 1),
        *pieces_of(7, 2), *pieces_of(8, 2), *pieces_of(9, 2), *pieces_of(6, 4),
    ]
    near, near_units = [up, down], [(0, 0, 1, 0, 768)]

    low_m, high_p = send(low, Z_UP), send(high, Z_DOWN)
    high_m, low_p = send(high, Z_UP), send(low, Z_DOWN)
    t_2u, t_2d = send(low_m, Z_UP), send(high_p, Z_DOWN)

    def both_cores(*values):
        return list(values) + [send(value, CORE) for value in values]

    own = both_cores(low, high)
    side = both_cores(low_m, high_m, low_p, high_p)
    far_z = both_cores(t_2u, t_2d)
    y_own = ffn(own, near, near_units)
    y_side = ffn(side, near, near_units)
    y_far = ffn(far_z, near, near_units)
    far_mine, far_other = ffn(far_z, far, far_units, y_far, (128, 128))
    m_mine, p_mine, m_other, p_other = ffn(side, far, far_units, y_side, (128, 128, 128, 128))
    own_mine, own_other = ffn(own, far, far_units, y_own, (128, 128))

    def plus(*values):
        return functools.reduce(lambda a, b: a + b, [value.astype(F32) for value in values])

    far_sum = plus(far_mine, send(far_other, CORE)).astype(BF16)
    to_p, to_m = send(far_sum[:64], Z_UP), send(far_sum[64:], Z_DOWN)
    low, high = ((0, 64), (0, 0)), ((64, 0), (0, 0))
    p_all = plus(p_mine, send(p_other, CORE), jnp.pad(to_p, low)).astype(BF16)
    m_all = plus(m_mine, send(m_other, CORE), jnp.pad(to_m, high)).astype(BF16)
    from_m, from_p = send(p_all, Z_UP), send(m_all, Z_DOWN)
    own_core = send(own_other, CORE)
    live = jnp.arange(128, dtype=jnp.int32) < lengths[0, 0]
    combined = plus(states, own_mine, own_core, from_m, from_p)
    return jnp.where(live[:, None], combined, 0.0).astype(BF16)[None, None]


def solution(mesh):
    placed = (
        P("req", "grp", None, None),
        P("req", "grp", None, None, None),
        P("req", "grp", None, None, None),
        P(),
        P("req", "grp"),
        P(),
        P("grp", None),
        P("grp", None),
    )
    return jax.shard_map(body, mesh=mesh, in_specs=placed, out_specs=P("req", "grp", None, None), check_vma=False)
```

```python
import functools
import math

import jax
import jax.numpy as jnp
import numpy as np
from jax import lax
from jax.experimental import pallas as pl
from jax.experimental.pallas import tpu as pltpu
from jax.sharding import PartitionSpec as P


HEADS = 32
NORM_EPS = 1e-05
AXES = ("req", "grp")
F32, BF16 = jnp.float32, jnp.bfloat16
MIB = 1024 * 1024


def pairs(move):
    table = []
    for r in range(8):
        for g in range(16):
            xl, y, z, xh, c = r // 4, r % 4, g // 4, (g // 2) % 2, g % 2
            a, b, d, e, f = move(xl, y, z, xh, c)
            table.append((r * 16 + g, (a * 4 + b % 4) * 16 + (d % 4) * 4 + e * 2 + f))
    return tuple(table)


Z_UP = pairs(lambda xl, y, z, xh, c: (xl, y, z + 1, xh, c))
Z_DOWN = pairs(lambda xl, y, z, xh, c: (xl, y, z - 1, xh, c))
Y_UP = pairs(lambda xl, y, z, xh, c: (xl, y + 1, z, xh, c))
Y_DOWN = pairs(lambda xl, y, z, xh, c: (xl, y - 1, z, xh, c))
X_LOW = pairs(lambda xl, y, z, xh, c: (1 - xl, y, z, xh, c))
X_CUT = pairs(lambda xl, y, z, xh, c: (1 - xl, y, z, 1 - xh, c))
CORE = pairs(lambda xl, y, z, xh, c: (xl, y, z, xh, 1 - c))


def req_offset(dx, dy):
    return pairs(lambda xl, y, z, xh, c: ((xl + dx) % 2, y + dy, z, xh, c))


OFFSETS = ((0, 0), (1, 2), (0, 2), (1, 1), (1, 3), (0, 1), (0, 3), (1, 0))


def send(value, table):
    return lax.ppermute(value, AXES, table)


def vmem():
    return pl.BlockSpec(memory_space=pltpu.VMEM)


def smem():
    return pl.BlockSpec(memory_space=pltpu.SMEM)


def hbm():
    return pl.BlockSpec(memory_space=pl.ANY)


def params(mib):
    return pltpu.CompilerParams(vmem_limit_bytes=mib * MIB)


def cost(flops, nbytes):
    return pl.CostEstimate(flops=int(flops), bytes_accessed=int(nbytes), transcendentals=0)


def cut_kernel(index_ref, cache_ref, *outs):
    for place, out in enumerate(outs):
        out[...] = cache_ref[pl.ds(pl.multiple_of(index_ref[place] * 32, 32), 32), :]


def cut_slices(index, cache):
    width = cache.shape[1]
    return pl.pallas_call(
        cut_kernel,
        out_shape=[jax.ShapeDtypeStruct((32, width), BF16)] * 8,
        in_specs=[smem(), vmem()],
        out_specs=[vmem()] * 8,
        compiler_params=params(8),
        cost_estimate=cost(0, 4 * cache.size),
        name="cut_slices",
    )(index, cache)


def share_kernel(index_ref, up_ref, down_ref, first_ref, second_ref, direct_ref, sems):
    start = index_ref[8] * 64
    moves = []

    def move(source, row, target, place, count):
        copy = pltpu.make_async_copy(
            source.at[pl.ds(row, count), :], target.at[pl.ds(place, count), :], sems.at[len(moves)]
        )
        copy.start()
        moves.append(copy)

    for i, target in enumerate((first_ref, second_ref)):
        row = pl.multiple_of(start + 32 * i, 32)
        move(up_ref, row, target, 0, 32)
        move(down_ref, row, target, 32, 32)
    move(up_ref, 512, direct_ref, 0, 256)
    move(down_ref, 512, direct_ref, 256, 256)
    for copy in moves:
        copy.wait()


def weight_shares(index, up, down):
    width = up.shape[1]
    return pl.pallas_call(
        share_kernel,
        out_shape=[jax.ShapeDtypeStruct((count, width), BF16) for count in (64, 64, 512)],
        in_specs=[smem(), hbm(), hbm()],
        out_specs=[vmem()] * 3,
        scratch_shapes=[pltpu.SemaphoreType.DMA((6,))],
        compiler_params=params(10),
        cost_estimate=cost(0, 4 * 640 * width),
        name="weight_shares",
    )(index, up, down)


GROUP = 8


def attention_kernel(slope_ref, place_ref, proj_ref, residual_ref, gain_ref, *refs):
    pieces, (state_ref, low_ref, high_ref, cached, bias, sums) = refs[:8], refs[8:]
    for place in range(8):
        cached[pl.ds(pl.multiple_of(place_ref[9 + place] * 32, 32), 32), :] = pieces[place][...]
    row = lax.broadcasted_iota(jnp.int32, (128, 256), 0)
    col = lax.broadcasted_iota(jnp.int32, (128, 256), 1)
    bias[...] = jnp.where(col - 128 <= row, (col - 128 - row).astype(F32), -1e30)
    sums[...] = jnp.zeros((128, 128), F32)
    ones = jnp.ones((256, 128), BF16)

    @pl.loop(0, HEADS // GROUP)
    def _(i):
        for j in range(GROUP):
            h = i * GROUP + j
            part = pl.ds(pl.multiple_of(h * 128, 128), 128)
            key = jnp.concatenate([cached[0:128, part], proj_ref[1, :, part]], axis=0)
            value = jnp.concatenate([cached[128:256, part], proj_ref[2, :, part]], axis=0)
            value = jnp.concatenate([value, ones], axis=1)
            scores = lax.dot_general(
                proj_ref[0, :, part], key, (((1,), (1,)), ((), ())), preferred_element_type=F32
            )
            scores = scores * (1.0 / math.sqrt(128)) + slope_ref[h] * bias[...]
            top = jnp.max(jnp.maximum(scores[:, :128], scores[:, 128:]), axis=1, keepdims=True)
            weights = jnp.exp(scores - top).astype(BF16)
            both = jnp.dot(weights, value, preferred_element_type=F32)
            state = (residual_ref[:, part].astype(F32) + both[:, :128] / both[:, 128:]).astype(BF16)
            state_ref[:, part] = state
            sums[...] += state.astype(F32)

    width = state_ref.shape[1]
    mean = jnp.broadcast_to(jnp.sum(sums[...], axis=1, keepdims=True) * (1.0 / width), (128, 128))
    squares = jnp.zeros((128, 128), F32)
    for h in range(HEADS):
        part = slice(h * 128, (h + 1) * 128)
        center = state_ref[:, part].astype(F32) - mean
        squares = squares + center * center
    spread = lax.rsqrt(jnp.sum(squares, axis=1, keepdims=True) * (1.0 / width) + NORM_EPS)
    spread = jnp.broadcast_to(spread, (128, 128))
    for h in range(HEADS):
        part = slice(h * 128, (h + 1) * 128)
        center = state_ref[:, part].astype(F32) - mean
        normed = (center * spread * gain_ref[:, part]).astype(BF16)
        low_ref[:, part] = normed[:64]
        high_ref[:, part] = normed[64:]


def attention(slopes, places, proj, residual, gain, pieces):
    width = proj.shape[2]
    return pl.pallas_call(
        attention_kernel,
        out_shape=[jax.ShapeDtypeStruct((128, width), BF16)] + [jax.ShapeDtypeStruct((64, width), BF16)] * 2,
        in_specs=[smem(), smem()] + [vmem()] * 11,
        out_specs=[vmem()] * 3,
        scratch_shapes=[pltpu.VMEM((256, width), BF16)]
        + [pltpu.VMEM((128, 256), F32), pltpu.VMEM((128, 128), F32)],
        compiler_params=params(20),
        cost_estimate=cost(8 * 128 * 256 * width, 8 * 128 * width * 2),
        name="attention",
    )(slopes, places, proj, residual, gain.reshape(1, width), *pieces)


UNIT_TILE = 256
COLUMN_TILE = 1024


def unit_copies(units):
    ups, downs, filled = [], [], 0
    for up_at, up_row, down_at, down_row, count in units:
        done = 0
        while done < count:
            take = min(count - done, UNIT_TILE - filled % UNIT_TILE)
            ups.append((up_at, up_row + done, take, filled))
            downs.append((down_at, down_row + done, take, filled))
            done += take
            filled += take
    return ups, downs, filled


def ffn_kernel(token_rows, source_count, ups, downs, with_acc, split, *refs):
    tokens = refs[: len(token_rows)]
    sources = refs[len(token_rows) : len(token_rows) + source_count]
    rest = refs[len(token_rows) + source_count :]
    start_ref = rest[0] if with_acc else None
    rest = rest[1:] if with_acc else rest
    out_count = len(split)
    outs = rest[:out_count]
    rows_buf, up_buf, down_buf, hidden, acc, result, token_sem, up_sem, down_sem, acc_sem, out_sem = rest[out_count:]
    _, width = rows_buf.shape
    at = 0
    moves = []
    for i, count in enumerate(token_rows):
        move = pltpu.make_async_copy(tokens[i], rows_buf.at[pl.ds(at, count), :], token_sem.at[i])
        move.start()
        moves.append(move)
        at += count
    for index, row, count, place in ups:
        pltpu.make_async_copy(
            sources[index].at[pl.ds(row, count), :], up_buf.at[pl.ds(place, count), :], up_sem.at[place // UNIT_TILE]
        ).start()
    for index, row, count, place in downs:
        pltpu.make_async_copy(
            sources[index].at[pl.ds(row, count), :], down_buf.at[pl.ds(place, count), :], down_sem
        ).start()
    if with_acc:
        begin = pltpu.make_async_copy(start_ref, acc, acc_sem)
        begin.start()
    for move in moves:
        move.wait()

    @pl.loop(0, up_buf.shape[0] // UNIT_TILE)
    def _(tile):
        part = pl.ds(pl.multiple_of(tile * UNIT_TILE, UNIT_TILE), UNIT_TILE)
        pltpu.make_async_copy(up_buf.at[part, :], up_buf.at[part, :], up_sem.at[tile]).wait()
        pre = lax.dot_general(
            rows_buf[...], up_buf[part, :], (((1,), (1,)), ((), ())), preferred_element_type=F32
        )
        hidden[:, part] = (0.5 * pre * (1.0 + lax.erf(pre * math.sqrt(0.5)))).astype(BF16)

    pltpu.make_async_copy(down_buf, down_buf, down_sem).wait()
    if with_acc:
        begin.wait()

    def stores(n):
        cols = pl.ds(pl.multiple_of(n * COLUMN_TILE, COLUMN_TILE), COLUMN_TILE)
        at = 0
        for i, count in enumerate(split):
            yield pltpu.make_async_copy(result.at[pl.ds(at, count), cols], outs[i].at[:, cols], out_sem.at[n, i])
            at += count

    @pl.loop(0, width // COLUMN_TILE)
    def _(n):
        cols = pl.ds(pl.multiple_of(n * COLUMN_TILE, COLUMN_TILE), COLUMN_TILE)
        value = jnp.dot(hidden[...], down_buf[:, cols], preferred_element_type=F32)
        if with_acc:
            value = value + acc[:, cols]
        result[:, cols] = value.astype(result.dtype)
        for copy in stores(n):
            copy.start()

    @pl.loop(0, width // COLUMN_TILE)
    def _(n):
        for copy in stores(n):
            copy.wait()


def ffn(tokens, arrays, units, start=None, split=None):
    ups, downs, filled = unit_copies(units)
    rows = tuple(token.shape[0] for token in tokens)
    total, width = sum(rows), tokens[0].shape[1]
    kind = BF16 if split else F32
    split = split or (total,)
    result = pl.pallas_call(
        functools.partial(ffn_kernel, rows, len(arrays), ups, downs, start is not None, split),
        out_shape=[jax.ShapeDtypeStruct((count, width), kind) for count in split],
        in_specs=[hbm()] * (len(tokens) + len(arrays) + (start is not None)),
        out_specs=[hbm()] * len(split),
        scratch_shapes=[
            pltpu.VMEM((total, width), BF16),
            pltpu.VMEM((filled, width), BF16),
            pltpu.VMEM((filled, width), BF16),
            pltpu.VMEM((total, filled), BF16),
            pltpu.VMEM((total if start is not None else 8, width), F32),
            pltpu.VMEM((total, width), kind),
            pltpu.SemaphoreType.DMA((len(tokens),)),
            pltpu.SemaphoreType.DMA((filled // UNIT_TILE,)),
            pltpu.SemaphoreType.DMA,
            pltpu.SemaphoreType.DMA,
            pltpu.SemaphoreType.DMA((width // COLUMN_TILE, len(split))),
        ],
        compiler_params=params(14 + total // 256 * 10),
        cost_estimate=cost(4 * total * filled * width, 2 * total * width * 3 + 4 * filled * width),
    )(*tokens, *arrays, *(() if start is None else (start,)))
    return result if len(split) > 1 else result[0]


def body(residual, suffix_proj, prefix_cache, owner_req, lengths, norm_gain, up, down):
    width = residual.shape[3]
    me = lax.axis_index("req")
    group = lax.axis_index("grp")
    xl, y = me // 4, me % 4
    owner = lax.dynamic_index_in_dim(owner_req, group, 0, keepdims=False)
    slopes = jnp.asarray(np.exp2(-8.0 * np.arange(1, HEADS + 1) / HEADS), F32)

    other = (1 - xl) * 4 + y
    dests = [((xl + dx) % 2) * 4 + (y + dy) % 4 for dx, dy in OFFSETS]
    origins = [((xl + dx) % 2) * 4 + (y - dy) % 4 for dx, dy in OFFSETS]
    index = jnp.stack(dests + [other] + origins).astype(jnp.int32)
    cuts = cut_slices(index, prefix_cache.reshape(256, width))
    kept = cuts[0]
    for place in range(1, 8):
        got = send(cuts[place], req_offset(*OFFSETS[place]))
        kept = jnp.where(origins[place] == owner, got, kept)
    pieces = [kept] + [send(kept, req_offset(*OFFSETS[place])) for place in range(1, 8)]

    first, second, direct = weight_shares(index, up, down)
    first, second = send(first, X_CUT), send(second, X_CUT)
    direct = send(direct, X_CUT)

    states, low, high = attention(slopes, index, suffix_proj[0, 0], residual[0, 0], norm_gain, pieces)

    a_own, b_own, _ = lax.optimization_barrier((first, second, tuple(pieces)))
    a_x = send(a_own, X_LOW)
    b_m, b_p = send(b_own, Y_UP), send(b_own, Y_DOWN)
    b_2 = send(b_own, req_offset(0, 2))
    b_x = send(jnp.concatenate([b_own, b_m, b_p, b_2]), X_LOW)
    a_pair = jnp.concatenate([a_own, a_x])
    a_m, a_p = send(a_pair, Y_UP), send(a_pair, Y_DOWN)
    a_2 = send(a_pair, req_offset(0, 2))
    far = [a_own, b_own, direct, a_x, b_m, b_p, b_2, b_x, a_m, a_p, a_2]
    pieces_of = lambda index, count: [(index, 64 * i, index, 64 * i + 32, 32) for i in range(count)]
    far_units = [
        *pieces_of(0, 1), *pieces_of(1, 1), (2, 0, 2, 256, 256), *pieces_of(3, 1), *pieces_of(4, 1), *pieces_of(5, 1),
        *pieces_of(6, 1), *pieces_of(8, 2), *pieces_of(9, 2), *pieces_of(10, 2), *pieces_of(7, 4),
    ]
    near, near_units = [up, down], [(0, 0, 1, 0, 768)]

    low_m, high_p = send(low, Z_UP), send(high, Z_DOWN)
    high_m, low_p = send(high, Z_UP), send(low, Z_DOWN)
    t_2u, t_2d = send(low_m, Z_UP), send(high_p, Z_DOWN)

    def both_cores(*values):
        return list(values) + [send(value, CORE) for value in values]

    own = both_cores(low, high)
    side = both_cores(low_m, high_m, low_p, high_p)
    far_z = both_cores(t_2u, t_2d)
    y_own = ffn(own, near, near_units)
    y_side = ffn(side, near, near_units)
    y_far = ffn(far_z, near, near_units)
    far_mine, far_other = ffn(far_z, far, far_units, y_far, (128, 128))
    m_mine, p_mine, m_other, p_other = ffn(side, far, far_units, y_side, (128, 128, 128, 128))
    own_mine, own_other = ffn(own, far, far_units, y_own, (128, 128))

    def plus(*values):
        return functools.reduce(lambda a, b: a + b, [value.astype(F32) for value in values])

    far_sum = plus(far_mine, send(far_other, CORE)).astype(BF16)
    to_p, to_m = send(far_sum[:64], Z_UP), send(far_sum[64:], Z_DOWN)
    low, high = ((0, 64), (0, 0)), ((64, 0), (0, 0))
    p_all = plus(p_mine, send(p_other, CORE), jnp.pad(to_p, low)).astype(BF16)
    m_all = plus(m_mine, send(m_other, CORE), jnp.pad(to_m, high)).astype(BF16)
    from_m, from_p = send(p_all, Z_UP), send(m_all, Z_DOWN)
    own_core = send(own_other, CORE)
    live = jnp.arange(128, dtype=jnp.int32) < lengths[0, 0]
    combined = plus(states, own_mine, own_core, from_m, from_p)
    return jnp.where(live[:, None], combined, 0.0).astype(BF16)[None, None]


def solution(mesh):
    placed = (
        P("req", "grp", None, None),
        P("req", "grp", None, None, None),
        P("req", "grp", None, None, None),
        P(),
        P("req", "grp"),
        P(),
        P("grp", None),
        P("grp", None),
    )
    return jax.shard_map(body, mesh=mesh, in_specs=placed, out_specs=P("req", "grp", None, None), check_vma=False)
```

```python
import functools
import math

import jax
import jax.numpy as jnp
import numpy as np
from jax import lax
from jax.experimental import pallas as pl
from jax.experimental.pallas import tpu as pltpu
from jax.sharding import PartitionSpec as P


HEADS = 32
NORM_EPS = 1e-05
AXES = ("req", "grp")
F32, BF16 = jnp.float32, jnp.bfloat16
MIB = 1024 * 1024


def pairs(move):
    table = []
    for r in range(8):
        for g in range(16):
            xl, y, z, xh, c = r // 4, r % 4, g // 4, (g // 2) % 2, g % 2
            a, b, d, e, f = move(xl, y, z, xh, c)
            table.append((r * 16 + g, (a * 4 + b % 4) * 16 + (d % 4) * 4 + e * 2 + f))
    return tuple(table)


Z_UP = pairs(lambda xl, y, z, xh, c: (xl, y, z + 1, xh, c))
Z_DOWN = pairs(lambda xl, y, z, xh, c: (xl, y, z - 1, xh, c))
Y_UP = pairs(lambda xl, y, z, xh, c: (xl, y + 1, z, xh, c))
Y_DOWN = pairs(lambda xl, y, z, xh, c: (xl, y - 1, z, xh, c))
X_LOW = pairs(lambda xl, y, z, xh, c: (1 - xl, y, z, xh, c))
X_CUT = pairs(lambda xl, y, z, xh, c: (1 - xl, y, z, 1 - xh, c))
CORE = pairs(lambda xl, y, z, xh, c: (xl, y, z, xh, 1 - c))


def req_offset(dx, dy):
    return pairs(lambda xl, y, z, xh, c: ((xl + dx) % 2, y + dy, z, xh, c))


OFFSETS = ((0, 0), (1, 2), (0, 2), (1, 1), (1, 3), (0, 1), (0, 3), (1, 0))


def send(value, table):
    return lax.ppermute(value, AXES, table)


def vmem():
    return pl.BlockSpec(memory_space=pltpu.VMEM)


def smem():
    return pl.BlockSpec(memory_space=pltpu.SMEM)


def hbm():
    return pl.BlockSpec(memory_space=pl.ANY)


def params(mib):
    return pltpu.CompilerParams(vmem_limit_bytes=mib * MIB)


def cost(flops, nbytes):
    return pl.CostEstimate(flops=int(flops), bytes_accessed=int(nbytes), transcendentals=0)


def cut_kernel(index_ref, cache_ref, *outs):
    for place, out in enumerate(outs):
        out[...] = cache_ref[pl.ds(pl.multiple_of(index_ref[place] * 32, 32), 32), :]


def cut_slices(index, cache):
    width = cache.shape[1]
    return pl.pallas_call(
        cut_kernel,
        out_shape=[jax.ShapeDtypeStruct((32, width), BF16)] * 8,
        in_specs=[smem(), vmem()],
        out_specs=[vmem()] * 8,
        compiler_params=params(8),
        cost_estimate=cost(0, 4 * cache.size),
        name="cut_slices",
    )(index, cache)


def share_kernel(index_ref, up_ref, down_ref, first_ref, second_ref, direct_ref, sems):
    start = index_ref[8] * 64
    moves = []

    def move(source, row, target, place, count):
        copy = pltpu.make_async_copy(
            source.at[pl.ds(row, count), :], target.at[pl.ds(place, count), :], sems.at[len(moves)]
        )
        copy.start()
        moves.append(copy)

    for i, target in enumerate((first_ref, second_ref)):
        row = pl.multiple_of(start + 32 * i, 32)
        move(up_ref, row, target, 0, 32)
        move(down_ref, row, target, 32, 32)
    move(up_ref, 512, direct_ref, 0, 256)
    move(down_ref, 512, direct_ref, 256, 256)
    for copy in moves:
        copy.wait()


def weight_shares(index, up, down):
    width = up.shape[1]
    return pl.pallas_call(
        share_kernel,
        out_shape=[jax.ShapeDtypeStruct((count, width), BF16) for count in (64, 64, 512)],
        in_specs=[smem(), hbm(), hbm()],
        out_specs=[vmem()] * 3,
        scratch_shapes=[pltpu.SemaphoreType.DMA((6,))],
        compiler_params=params(58),
        cost_estimate=cost(0, 4 * 640 * width),
        name="weight_shares",
    )(index, up, down)


GROUP = 8


def attention_kernel(slope_ref, place_ref, proj_ref, residual_ref, gain_ref, *refs):
    pieces, (state_ref, low_ref, high_ref, cached, bias, sums) = refs[:8], refs[8:]
    for place in range(8):
        cached[pl.ds(pl.multiple_of(place_ref[9 + place] * 32, 32), 32), :] = pieces[place][...]
    row = lax.broadcasted_iota(jnp.int32, (128, 256), 0)
    col = lax.broadcasted_iota(jnp.int32, (128, 256), 1)
    bias[...] = jnp.where(col - 128 <= row, (col - 128 - row).astype(F32), -1e30)
    sums[...] = jnp.zeros((128, 128), F32)
    ones = jnp.ones((256, 128), BF16)

    @pl.loop(0, HEADS // GROUP)
    def _(i):
        for j in range(GROUP):
            h = i * GROUP + j
            part = pl.ds(pl.multiple_of(h * 128, 128), 128)
            key = jnp.concatenate([cached[0:128, part], proj_ref[1, :, part]], axis=0)
            value = jnp.concatenate([cached[128:256, part], proj_ref[2, :, part]], axis=0)
            value = jnp.concatenate([value, ones], axis=1)
            scores = lax.dot_general(
                proj_ref[0, :, part], key, (((1,), (1,)), ((), ())), preferred_element_type=F32
            )
            scores = scores * (1.0 / math.sqrt(128)) + slope_ref[h] * bias[...]
            top = jnp.max(jnp.maximum(scores[:, :128], scores[:, 128:]), axis=1, keepdims=True)
            weights = jnp.exp(scores - top).astype(BF16)
            both = jnp.dot(weights, value, preferred_element_type=F32)
            state = (residual_ref[:, part].astype(F32) + both[:, :128] / both[:, 128:]).astype(BF16)
            state_ref[:, part] = state
            sums[...] += state.astype(F32)

    width = state_ref.shape[1]
    mean = jnp.broadcast_to(jnp.sum(sums[...], axis=1, keepdims=True) * (1.0 / width), (128, 128))
    squares = jnp.zeros((128, 128), F32)
    for h in range(HEADS):
        part = slice(h * 128, (h + 1) * 128)
        center = state_ref[:, part].astype(F32) - mean
        squares = squares + center * center
    spread = lax.rsqrt(jnp.sum(squares, axis=1, keepdims=True) * (1.0 / width) + NORM_EPS)
    spread = jnp.broadcast_to(spread, (128, 128))
    for h in range(HEADS):
        part = slice(h * 128, (h + 1) * 128)
        center = state_ref[:, part].astype(F32) - mean
        normed = (center * spread * gain_ref[:, part]).astype(BF16)
        low_ref[:, part] = normed[:64]
        high_ref[:, part] = normed[64:]


def attention(slopes, places, proj, residual, gain, pieces):
    width = proj.shape[2]
    return pl.pallas_call(
        attention_kernel,
        out_shape=[jax.ShapeDtypeStruct((128, width), BF16)] + [jax.ShapeDtypeStruct((64, width), BF16)] * 2,
        in_specs=[smem(), smem()] + [vmem()] * 11,
        out_specs=[vmem()] * 3,
        scratch_shapes=[pltpu.VMEM((256, width), BF16)]
        + [pltpu.VMEM((128, 256), F32), pltpu.VMEM((128, 128), F32)],
        compiler_params=params(20),
        cost_estimate=cost(8 * 128 * 256 * width, 8 * 128 * width * 2),
        name="attention",
    )(slopes, places, proj, residual, gain.reshape(1, width), *pieces)


UNIT_TILE = 256
COLUMN_TILE = 1024


def unit_copies(units):
    ups, downs, filled = [], [], 0
    for up_at, up_row, down_at, down_row, count in units:
        done = 0
        while done < count:
            take = min(count - done, UNIT_TILE - filled % UNIT_TILE)
            ups.append((up_at, up_row + done, take, filled))
            downs.append((down_at, down_row + done, take, filled))
            done += take
            filled += take
    return ups, downs, filled


def ffn_kernel(token_rows, source_count, ups, downs, with_acc, split, *refs):
    tokens = refs[: len(token_rows)]
    sources = refs[len(token_rows) : len(token_rows) + source_count]
    rest = refs[len(token_rows) + source_count :]
    start_ref = rest[0] if with_acc else None
    rest = rest[1:] if with_acc else rest
    outs = rest[: len(split)]
    rest = rest[len(split) :]
    up_buf, down_buf = sources if not ups else rest[:2]
    rest = rest if not ups else rest[2:]
    rows_buf, hidden, acc, result, token_sem, up_sem, down_sem, acc_sem, out_sem = rest
    _, width = rows_buf.shape
    at = 0
    moves = []
    for i, count in enumerate(token_rows):
        move = pltpu.make_async_copy(tokens[i], rows_buf.at[pl.ds(at, count), :], token_sem.at[i])
        move.start()
        moves.append(move)
        at += count
    for index, row, count, place in ups:
        pltpu.make_async_copy(
            sources[index].at[pl.ds(row, count), :], up_buf.at[pl.ds(place, count), :], up_sem.at[place // UNIT_TILE]
        ).start()
    for index, row, count, place in downs:
        pltpu.make_async_copy(
            sources[index].at[pl.ds(row, count), :], down_buf.at[pl.ds(place, count), :], down_sem
        ).start()
    if with_acc:
        begin = pltpu.make_async_copy(start_ref, acc, acc_sem)
        begin.start()
    for move in moves:
        move.wait()

    @pl.loop(0, up_buf.shape[0] // UNIT_TILE)
    def _(tile):
        part = pl.ds(pl.multiple_of(tile * UNIT_TILE, UNIT_TILE), UNIT_TILE)
        if ups:
            pltpu.make_async_copy(up_buf.at[part, :], up_buf.at[part, :], up_sem.at[tile]).wait()
        pre = lax.dot_general(
            rows_buf[...], up_buf[part, :], (((1,), (1,)), ((), ())), preferred_element_type=F32
        )
        hidden[:, part] = (0.5 * pre * (1.0 + lax.erf(pre * math.sqrt(0.5)))).astype(BF16)

    if downs:
        pltpu.make_async_copy(down_buf, down_buf, down_sem).wait()
    if with_acc:
        begin.wait()

    def stores(n):
        cols = pl.ds(pl.multiple_of(n * COLUMN_TILE, COLUMN_TILE), COLUMN_TILE)
        at = 0
        for i, count in enumerate(split):
            yield pltpu.make_async_copy(result.at[pl.ds(at, count), cols], outs[i].at[:, cols], out_sem.at[n, i])
            at += count

    @pl.loop(0, width // COLUMN_TILE)
    def _(n):
        cols = pl.ds(pl.multiple_of(n * COLUMN_TILE, COLUMN_TILE), COLUMN_TILE)
        value = jnp.dot(hidden[...], down_buf[:, cols], preferred_element_type=F32)
        if with_acc:
            value = value + acc[:, cols]
        result[:, cols] = value.astype(result.dtype)
        for copy in stores(n):
            copy.start()

    @pl.loop(0, width // COLUMN_TILE)
    def _(n):
        for copy in stores(n):
            copy.wait()


def ffn(tokens, arrays, units, start=None, split=None):
    ups, downs, filled = unit_copies(units) if units else ((), (), arrays[0].shape[0])
    source = pl.BlockSpec(memory_space=pltpu.HBM) if units else vmem()
    rows = tuple(token.shape[0] for token in tokens)
    total, width = sum(rows), tokens[0].shape[1]
    kind = BF16 if split else F32
    split = split or (total,)
    result = pl.pallas_call(
        functools.partial(ffn_kernel, rows, len(arrays), ups, downs, start is not None, split),
        out_shape=[jax.ShapeDtypeStruct((count, width), kind) for count in split],
        in_specs=[hbm()] * len(tokens) + [source] * len(arrays) + [hbm()] * (start is not None),
        out_specs=[hbm()] * len(split),
        scratch_shapes=[pltpu.VMEM((filled, width), BF16)] * (2 if units else 0)
        + [
            pltpu.VMEM((total, width), BF16),
            pltpu.VMEM((total, filled), BF16),
            pltpu.VMEM((total if start is not None else 8, width), F32),
            pltpu.VMEM((total, width), kind),
            pltpu.SemaphoreType.DMA((len(tokens),)),
            pltpu.SemaphoreType.DMA((filled // UNIT_TILE,)),
            pltpu.SemaphoreType.DMA,
            pltpu.SemaphoreType.DMA,
            pltpu.SemaphoreType.DMA((width // COLUMN_TILE, len(split))),
        ],
        compiler_params=params((14 if units else 1) + total // 256 * 9),
        cost_estimate=cost(4 * total * filled * width, 2 * total * width * 3 + 4 * filled * width),
    )(*tokens, *arrays, *(() if start is None else (start,)))
    return result if len(split) > 1 else result[0]


def body(residual, suffix_proj, prefix_cache, owner_req, lengths, norm_gain, up, down):
    width = residual.shape[3]
    me = lax.axis_index("req")
    group = lax.axis_index("grp")
    xl, y = me // 4, me % 4
    owner = lax.dynamic_index_in_dim(owner_req, group, 0, keepdims=False)
    slopes = jnp.asarray(np.exp2(-8.0 * np.arange(1, HEADS + 1) / HEADS), F32)

    other = (1 - xl) * 4 + y
    dests = [((xl + dx) % 2) * 4 + (y + dy) % 4 for dx, dy in OFFSETS]
    origins = [((xl + dx) % 2) * 4 + (y - dy) % 4 for dx, dy in OFFSETS]
    index = jnp.stack(dests + [other] + origins).astype(jnp.int32)
    cuts = cut_slices(index, prefix_cache.reshape(256, width))
    kept = cuts[0]
    for place in range(1, 8):
        got = send(cuts[place], req_offset(*OFFSETS[place]))
        kept = jnp.where(origins[place] == owner, got, kept)
    pieces = [kept] + [send(kept, req_offset(*OFFSETS[place])) for place in range(1, 8)]

    first, second, direct = weight_shares(index, up, down)
    first, second = send(first, X_CUT), send(second, X_CUT)
    direct = send(direct, X_CUT)

    states, low, high = attention(slopes, index, suffix_proj[0, 0], residual[0, 0], norm_gain, pieces)

    a_own, b_own, _ = lax.optimization_barrier((first, second, tuple(pieces)))
    two = req_offset(0, 2)
    b_m, b_p, b_2 = send(b_own, Y_UP), send(b_own, Y_DOWN), send(b_own, two)
    a_x, b_x0 = send(a_own, X_LOW), send(b_own, X_LOW)
    a_m, a_p, a_2 = send(a_own, Y_UP), send(a_own, Y_DOWN), send(a_own, two)
    b_x = send(jnp.concatenate([b_m, b_p, b_2]), X_LOW)
    a_xm, a_xp, a_x2 = send(a_x, Y_UP), send(a_x, Y_DOWN), send(a_x, two)
    far = [a_own, b_own, direct, a_x, b_m, b_p, b_2, b_x0, a_m, a_p, a_2, a_xm, a_xp, a_x2, b_x]
    pieces_of = lambda index, count: [(index, 64 * i, index, 64 * i + 32, 32) for i in range(count)]
    far_units = [
        *pieces_of(0, 1), *pieces_of(1, 1), (2, 0, 2, 256, 256),
        *(piece for index in range(3, 14) for piece in pieces_of(index, 1)), *pieces_of(14, 3),
    ]
    near, near_units = [up, down], ()

    low_m, high_p = send(low, Z_UP), send(high, Z_DOWN)
    high_m, low_p = send(high, Z_UP), send(low, Z_DOWN)
    t_2u, t_2d = send(low_m, Z_UP), send(high_p, Z_DOWN)

    def both_cores(*values):
        return list(values) + [send(value, CORE) for value in values]

    own = both_cores(low, high)
    side = both_cores(low_m, high_m, low_p, high_p)
    far_z = both_cores(t_2u, t_2d)
    y_own = ffn(own, near, near_units)
    y_side = ffn(side, near, near_units)
    y_far = ffn(far_z, near, near_units)
    far_mine, far_other = ffn(far_z, far, far_units, y_far, (128, 128))
    m_mine, p_mine, m_other, p_other = ffn(side, far, far_units, y_side, (128, 128, 128, 128))
    own_mine, own_other = ffn(own, far, far_units, y_own, (128, 128))

    def plus(*values):
        return functools.reduce(lambda a, b: a + b, [value.astype(F32) for value in values])

    far_sum = plus(far_mine, send(far_other, CORE)).astype(BF16)
    to_p, to_m = send(far_sum[:64], Z_UP), send(far_sum[64:], Z_DOWN)
    low, high = ((0, 64), (0, 0)), ((64, 0), (0, 0))
    p_all = plus(p_mine, send(p_other, CORE), jnp.pad(to_p, low)).astype(BF16)
    m_all = plus(m_mine, send(m_other, CORE), jnp.pad(to_m, high)).astype(BF16)
    from_m, from_p = send(p_all, Z_UP), send(m_all, Z_DOWN)
    own_core = send(own_other, CORE)
    live = jnp.arange(128, dtype=jnp.int32) < lengths[0, 0]
    combined = plus(states, own_mine, own_core, from_m, from_p)
    return jnp.where(live[:, None], combined, 0.0).astype(BF16)[None, None]


def solution(mesh):
    placed = (
        P("req", "grp", None, None),
        P("req", "grp", None, None, None),
        P("req", "grp", None, None, None),
        P(),
        P("req", "grp"),
        P(),
        P("grp", None),
        P("grp", None),
    )
    return jax.shard_map(body, mesh=mesh, in_specs=placed, out_specs=P("req", "grp", None, None), check_vma=False)
```
